512 devices in a mesh: wide: 64 (over y_lo, z, core), narrow: 8 (over x, y_hi).
Axes of the slice: x: 4, y: 4 (y_hi: 2, y_lo: 2; y = y_hi * 2 + y_lo), z: 16, core: 2. Of those that a mesh axis runs over, the one named last changes fastest.
Arguments:
- cell_rows: bfloat16 [32768, 2048], P('wide', 'narrow'), may hold values from -3 to 3
- attn_gain: float32 [2048], replicated, may hold values from 0.1 to 1.9
- ffn_gain: float32 [2048], replicated, may hold values from 0.1 to 1.9
- panels: bfloat16 [64, 2048, 4096], P('wide', None, 'narrow'), may hold values from -0.125 to 0.125
- panel_slot: int32 [64], replicated, may hold values from 0 to 63, each once
- layout: int32 [256, 3], P('wide'), may hold values from 0 to 31, as said below
Outputs:
- encoded: bfloat16 [32768, 2048], P('wide', 'narrow')
The draws below stay inside these ranges and needn't reach their ends.
Inputs may be any that keep to these rules, and one draw needn't show every extreme that they name: `panel_slot`: the first three entries name the indices of wide that hold this layer's attention panel, feed-forward input panel and feed-forward output panel; all entries differ. `layout`: row b lists the position p(b) of block b itself first, then two other positions of the same netlist at most 2 away; the three differ. One of the two lies before p(b) and one after it, except for the first two and last two positions of a netlist.
All inputs are finite; a program needn't handle non-finite values.
Results may differ from the reference program's by a relative error of at most 0.018.
Values may be sent and summed in bfloat16 or wider, within the bound.
A program may use at most 64 MiB of HBM per device.

```python
import jax
import jax.numpy as jnp
from jax import lax

D = 2048
HD = 128
HEADS = 8
BLK = 128
BLK_DEV = 4
NET_BLOCKS = 32
TOKENS = 32768
QBLOCKS = 256
PANEL = 4096
FFW = 4096
N_WIDE = 64
N_NARROW = 8


def draw_layout(key, part):
    position = (jnp.arange(QBLOCKS, dtype=jnp.int32) + BLK_DEV // 2) % NET_BLOCKS
    coins = jax.random.randint(key, (QBLOCKS, 2), 0, 2, dtype=jnp.int32)
    lower = -1 - coins[:, 0]
    upper = 1 + coins[:, 1]
    lower = jnp.where(position == 1, -1, lower)
    upper = jnp.where(position == NET_BLOCKS - 2, 1, upper)
    first = jnp.where(position == 0, 1, jnp.where(position == NET_BLOCKS - 1, -1, lower))
    second = jnp.where(position == 0, 2, jnp.where(position == NET_BLOCKS - 1, -2, upper))
    picked = jnp.stack([position, position + first, position + second], axis=1)
    return picked.astype(jnp.int32)


def block_levels(rng, dims, cuts, low, largest):
    factor_of, own = 1.0, jax.random.fold_in(rng, 6)
    for dim, shards_of in cuts:
        draws = jnp.exp(jax.random.uniform(jax.random.fold_in(own, dim), (shards_of,), jnp.float32, low / len(cuts), largest / len(cuts)))
        factor_of = factor_of * jnp.repeat(draws, dims[dim] // shards_of).reshape([-1 if axis == dim else 1 for axis in range(len(dims))])
    return factor_of


def gaussian(rng, dims, spread, most, split=(), held_as=jnp.bfloat16):
    values = jax.random.normal(rng, dims, jnp.float32) * spread
    if len(split) > 0:
        values = block_levels(rng, dims, split, -0.22, 0.18) * values
    return jnp.clip(values, min=-most, max=most).astype(held_as)


def setup_inputs(seed: int = 0) -> dict:
    arg_keys = jax.random.split(jax.random.key(seed), 7)
    cell_rows = gaussian(arg_keys[0], (TOKENS, D), 0.5, 3.0, ((0, 64), (1, 8)))
    attn_gain = jnp.clip(1.0 + 0.18 * jax.random.normal(arg_keys[1], (D,), jnp.float32), 0.1, 1.9)
    ffn_gain = jnp.clip(1.0 + 0.18 * jax.random.normal(arg_keys[2], (D,), jnp.float32), 0.1, 1.9)
    panels = gaussian(arg_keys[3], (N_WIDE, D, PANEL), D ** -0.5, 0.125, ((0, 64), (2, 8)))
    panel_slot = jax.random.permutation(arg_keys[4], N_WIDE).astype(jnp.int32)
    layout = draw_layout(jax.random.fold_in(arg_keys[6], 71), 0)
    return dict(cell_rows=cell_rows, attn_gain=attn_gain, ffn_gain=ffn_gain, panels=panels, panel_slot=panel_slot, layout=layout)


epsilon = 1e-05

def rms_scale(values, gain):
    mean_square = lax.optimization_barrier(jnp.mean(values * values, axis=-1, keepdims=True))
    return values * lax.rsqrt(mean_square + epsilon) * gain

def block_mask(layout, query_index):
    wanted = query_index[:, None] + jnp.arange(5, dtype=jnp.int32)[None, :] - 2
    return jnp.any(layout[:, :, None] == wanted[:, None, :], axis=1)

def attend(head_queries, head_keys, head_values, allowed):
    scores = jnp.einsum('bqc,bokc->bqok', head_queries.astype(jnp.float32), head_keys.astype(jnp.float32)) * HD ** (-0.5)
    lifted = jnp.where(allowed[:, None, :, None], jnp.exp(scores), jnp.float32(0.0))
    weights = (lifted / lax.optimization_barrier(jnp.sum(lifted, axis=(2, 3), keepdims=True))).astype(jnp.bfloat16)
    return jnp.einsum('bqok,bokc->bqc', weights.astype(jnp.float32), head_values.astype(jnp.float32)).astype(jnp.bfloat16)

def grouped_sum(left, right):

    def add_group(running, pieces):
        part = jnp.dot(pieces[0], pieces[1].T, preferred_element_type=jnp.float32).astype(jnp.bfloat16)
        part = lax.optimization_barrier(part)
        return (running + part.astype(jnp.float32), None)
    start = jnp.zeros((left.shape[1], right.shape[1]), jnp.float32)
    total, _ = lax.scan(add_group, start, (left, right))
    return total

def reference(cell_rows, attn_gain, ffn_gain, panels, panel_slot, layout):
    attn_panel = lax.dynamic_index_in_dim(panels, panel_slot[0], 0, keepdims=False)
    up_panel = lax.dynamic_index_in_dim(panels, panel_slot[1], 0, keepdims=False)
    down_panel = lax.dynamic_index_in_dim(panels, panel_slot[2], 0, keepdims=False)
    stream_in = cell_rows.astype(jnp.float32)
    normed = rms_scale(stream_in, attn_gain).astype(jnp.bfloat16)
    attn_table = attn_panel.reshape(D, HEADS, 4, HD)
    projected = jnp.einsum('td,dhjc->thjc', normed.astype(jnp.float32), attn_table[:, :, :3, :].astype(jnp.float32)).astype(jnp.bfloat16)
    block_count = TOKENS // BLK
    query_index = (jnp.arange(block_count, dtype=jnp.int32) + BLK_DEV // 2) % NET_BLOCKS
    allowed = block_mask(layout, query_index)
    padding = jnp.zeros((2 * BLK, HEADS, 2, HD), jnp.bfloat16)
    padded = jnp.concatenate([padding, projected[:, :, 1:, :], padding], axis=0)
    head_queries = projected[:, :, 0, :].reshape(block_count, BLK, HEADS, HD).transpose(2, 0, 1, 3)
    head_pairs = padded.reshape(block_count + 4, BLK, HEADS, 2, HD).transpose(2, 0, 1, 3, 4)

    def one_head(pieces):
        queries_here, pairs_here = pieces
        stacked = jnp.stack([pairs_here[offset:offset + block_count] for offset in range(5)], axis=1)
        return attend(queries_here, stacked[:, :, :, 0, :], stacked[:, :, :, 1, :], allowed)
    head_out = lax.map(one_head, (head_queries, head_pairs))
    head_out = head_out.transpose(1, 2, 0, 3).reshape(TOKENS, HEADS, HD)
    group_width = HEADS // N_NARROW * HD
    group_out = head_out.reshape(TOKENS, N_NARROW, group_width).transpose(1, 0, 2)
    out_rows = attn_table[:, :, 3, :].reshape(D, N_NARROW, group_width).transpose(1, 0, 2)
    attn_sum = grouped_sum(group_out, out_rows)
    stream = (stream_in + attn_sum).astype(jnp.bfloat16)
    normed_ffn = rms_scale(stream.astype(jnp.float32), ffn_gain).astype(jnp.bfloat16)
    hidden = jax.nn.gelu(jnp.dot(normed_ffn, up_panel, preferred_element_type=jnp.float32), approximate=False).astype(jnp.bfloat16)
    unit_width = FFW // N_NARROW
    group_hidden = hidden.reshape(TOKENS, N_NARROW, unit_width).transpose(1, 0, 2)
    group_down = down_panel.reshape(D, N_NARROW, unit_width).transpose(1, 0, 2)
    ffn_sum = grouped_sum(group_hidden, group_down)
    return (stream.astype(jnp.float32) + ffn_sum).astype(jnp.bfloat16)
```

```python
import functools

import jax
import jax.numpy as jnp
from jax import lax
from jax.experimental import pallas as pl
from jax.experimental.pallas import tpu as pltpu
from jax.sharding import PartitionSpec as P

HD = 128
BLK = 128
NET_BLOCKS = 32
NZ = 16
NW = 64
NN = 8
UP = 8
DOWN = 7
epsilon = 1e-05

BF = jnp.bfloat16
F32 = jnp.float32
VM = pl.BlockSpec(memory_space=pltpu.VMEM)
SM = pl.BlockSpec(memory_space=pltpu.SMEM)
DMA = pltpu.SemaphoreType.DMA
LIMIT = 60 * 1024 * 1024


def remote(src, dst, send, recv, wide, narrow):
    return pltpu.make_async_remote_copy(
        src_ref=src, dst_ref=dst, send_sem=send, recv_sem=recv,
        device_id=(wide, narrow), device_id_type=pl.DeviceIdType.MESH,
    )


def greet(devices):
    barrier = pltpu.get_barrier_semaphore()
    for wide, narrow in devices:
        pl.semaphore_signal(
            barrier, inc=1, device_id=(wide, narrow), device_id_type=pl.DeviceIdType.MESH
        )
    pl.semaphore_wait(barrier, len(devices))


def loop(low, high, body):
    def step(s, carry):
        body(s)
        return carry

    lax.fori_loop(low, high, step, 0)


def panels_and_cells(
    cell, panel, slot, gath, out0, out1, out2,
    cbuf, rsp, rsm, ysend, yrecv,
    own_sem, csem, nsend, nrecv, psend, precv, msend, mrecv, ysem,
    gpsend, gprecv, gmsend, gmrecv, xsend, xrecv,
):
    outs = (out0, out1, out2)
    w = lax.axis_index("wide")
    n = lax.axis_index("narrow")
    core = w % 2
    z = (w // 2) % NZ
    yl = w // (2 * NZ)
    chip = w // 2

    def at_z(zz):
        return (yl * NZ + (zz + NZ) % NZ) * 2 + core

    above, below = at_z(z + 1), at_z(z - 1)
    partner = w + 1 - 2 * core
    across = (w + 2 * NZ) % NW
    peers = [(n + k) % NN for k in range(1, NN)]
    greet(
        [(partner, n), (above, n), (below, n), (across, n)] + [(w, p) for p in peers]
    )
    to_partner = remote(panel.at[:, 1 - core], cbuf, csem.at[0], csem.at[1], partner, n)
    to_partner.start()
    columns = gath.at[:, pl.ds(pl.multiple_of(n * 256, 256), 256)]
    own = pltpu.make_async_copy(cell, columns, own_sem)
    own.start()
    sends = []
    for k in range(1, NN):
        copy = remote(cell, columns, nsend.at[k - 1], nrecv.at[k - 1], w, peers[k - 1])
        copy.start()
        sends.append(copy)
    to_partner.wait_recv()

    slots = [slot[i] for i in range(3)]

    def chip_data(i, j):
        return jnp.where(slots[i] % 2 == core, panel[j, core], cbuf[j])

    def up(s, i):
        return remote(rsp.at[s, i], rsp.at[s + 1, i], psend.at[s, i], precv.at[s, i], above, n)

    def down(s, i):
        return remote(rsm.at[s, i], rsm.at[s + 1, i], msend.at[s, i], mrecv.at[s, i], below, n)

    for i in range(3):
        rsp[0, i] = chip_data(i, (z + UP) % NZ)
        up(0, i).start()
        rsm[0, i] = chip_data(i, (z + NZ - DOWN) % NZ)
        down(0, i).start()

    def merge_up(s, i):
        up(s - 1, i).wait_recv()
        mine = chip_data(i, (z + UP - s) % NZ)
        rsp[s, i] = jnp.where(slots[i] // 2 == chip, mine, rsp[s, i])
        up(s, i).start()

    def merge_down(s, i):
        down(s - 1, i).wait_recv()
        mine = chip_data(i, (z + NZ - DOWN + s) % NZ)
        rsm[s, i] = jnp.where(slots[i] // 2 == chip, mine, rsm[s, i])
        down(s, i).start()

    def both(s):
        for i in range(3):
            merge_up(s, i)
            merge_down(s, i)

    loop(1, DOWN, both)
    for i in range(3):
        merge_up(UP - 1, i)

    def swap(i):
        return remote(ysend.at[i], yrecv.at[i], ysem.at[0, i], ysem.at[1, i], across, n)

    for i in range(3):
        up(UP - 1, i).wait_recv()
        down(DOWN - 1, i).wait_recv()
        behind = (z - (slots[i] // 2) % NZ + NZ) % NZ
        ring = jnp.where(behind <= UP, rsp[UP, i], rsm[DOWN, i])
        ysend[i] = jnp.where(slots[i] // 2 == chip, chip_data(i, z), ring)
        swap(i).start()

    def gather_up(s, i):
        part = outs[i].at[(z - s + NZ) % NZ, core]
        return remote(part, part, gpsend.at[s, i], gprecv.at[s, i], above, n)

    def gather_down(s, i):
        part = outs[i].at[(z + s) % NZ, core]
        return remote(part, part, gmsend.at[s, i], gmrecv.at[s, i], below, n)

    def hand(order, chunk, i):
        part = outs[i].at[(chunk + NZ) % NZ, core]
        return remote(part, part, xsend.at[order, i], xrecv.at[order, i], partner, n)

    for i in range(3):
        swap(i).wait_recv()
        outs[i][z, core] = jnp.where(slots[i] // (2 * NZ) == yl, ysend[i], yrecv[i])
        gather_up(0, i).start()
        gather_down(0, i).start()
        hand(0, z, i).start()

    def relay_up(s, i):
        gather_up(s - 1, i).wait_recv()
        gather_up(s, i).start()
        hand(s, z - s, i).start()

    def relay_down(s, i):
        gather_down(s - 1, i).wait_recv()
        gather_down(s, i).start()
        hand(UP + s, z + s, i).start()

    def relay(s):
        for i in range(3):
            relay_up(s, i)
            relay_down(s, i)

    loop(1, DOWN, relay)
    for i in range(3):
        relay_up(DOWN, i)
    for i in range(3):
        gather_up(UP - 1, i).wait_recv()
        hand(UP, z - UP, i).start()
        gather_down(DOWN - 1, i).wait_recv()
        hand(UP + DOWN, z + DOWN, i).start()

    own.wait()
    to_partner.wait_send()
    for copy in sends:
        copy.wait()

    def finish(s):
        for i in range(3):
            up(s, i).wait_send()
            gather_up(s, i).wait_send()

            @pl.when(s < DOWN)
            def _():
                down(s, i).wait_send()
                gather_down(s, i).wait_send()

    loop(0, UP, finish)
    for i in range(3):
        swap(i).wait_send()

    def handed(order):
        for i in range(3):
            hand(order, z, i).wait()

    loop(0, NZ, handed)


def gather_all(cell_rows, panel, panel_slot):
    rows, width = cell_rows.shape
    piece = (64, 512)
    big = jax.ShapeDtypeStruct((NZ, 2, 64, 512), BF)
    gath, *outs = pl.pallas_call(
        panels_and_cells,
        name="panels_and_cells",
        out_shape=[jax.ShapeDtypeStruct((rows, width * NN), BF), big, big, big],
        in_specs=[VM, VM, SM],
        out_specs=[VM] * 4,
        scratch_shapes=[
            pltpu.VMEM((NZ,) + piece, BF),
            pltpu.VMEM((UP + 1, 3) + piece, BF),
            pltpu.VMEM((DOWN + 1, 3) + piece, BF),
            pltpu.VMEM((3,) + piece, BF),
            pltpu.VMEM((3,) + piece, BF),
            DMA, DMA((2,)), DMA((NN - 1,)), DMA((NN - 1,)),
            DMA((UP, 3)), DMA((UP, 3)), DMA((DOWN, 3)), DMA((DOWN, 3)), DMA((2, 3)),
            DMA((UP, 3)), DMA((UP, 3)), DMA((DOWN, 3)), DMA((DOWN, 3)),
            DMA((NZ, 3)), DMA((NZ, 3)),
        ],
        compiler_params=pltpu.CompilerParams(
            collective_id=0, has_side_effects=True, vmem_limit_bytes=LIMIT
        ),
    )(cell_rows, panel.reshape((NZ, 2, 64, 512)), panel_slot)
    return gath, [o.reshape(2048, 512) for o in outs]


def scatter_rows(part, got, send, recv, own_sem, w, n, peers):
    def columns(p):
        return part.at[:, pl.ds(pl.multiple_of(p * 256, 256), 256)]

    copies = []
    for k in range(1, NN):
        copy = remote(
            columns(peers[k - 1]), got.at[k - 1], send.at[k - 1], recv.at[k - 1], w, peers[k - 1]
        )
        copy.start()
        copies.append(copy)
    own = pltpu.make_async_copy(columns(n), got.at[NN - 1], own_sem)
    own.start()
    own.wait()
    for copy in copies:
        copy.wait()


def summed(base, got, rows):
    total = got[0, rows].astype(F32)
    for k in range(1, NN):
        total = total + got[k, rows].astype(F32)
    return (base[rows].astype(F32) + total).astype(BF)


def reduce_and_gather(
    part, cell, stream, gath, got, send, recv, own_sem, send2, recv2
):
    w = lax.axis_index("wide")
    n = lax.axis_index("narrow")
    peers = [(n + k) % NN for k in range(1, NN)]
    greet([(w, p) for p in peers])
    scatter_rows(part, got, send, recv, own_sem, w, n, peers)

    def block(r):
        rows = pl.ds(pl.multiple_of(r * 64, 64), 64)
        stream[rows] = summed(cell, got, rows)

    loop(0, 8, block)
    columns = gath.at[:, pl.ds(pl.multiple_of(n * 256, 256), 256)]
    own = pltpu.make_async_copy(stream, columns, own_sem)
    own.start()
    copies = []
    for k in range(1, NN):
        copy = remote(stream, columns, send2.at[k - 1], recv2.at[k - 1], w, peers[k - 1])
        copy.start()
        copies.append(copy)
    own.wait()
    for copy in copies:
        copy.wait()


def reduce_only(part, base, encoded, got, send, recv, own_sem):
    w = lax.axis_index("wide")
    n = lax.axis_index("narrow")
    peers = [(n + k) % NN for k in range(1, NN)]
    greet([(w, p) for p in peers])
    scatter_rows(part, got, send, recv, own_sem, w, n, peers)

    def block(r):
        rows = pl.ds(pl.multiple_of(r * 64, 64), 64)
        encoded[rows] = summed(base, got, rows)

    loop(0, 8, block)


def call_reduce_and_gather(part, cell):
    rows, width = cell.shape
    sems = DMA((NN - 1,))
    return pl.pallas_call(
        reduce_and_gather,
        name="reduce_and_gather",
        out_shape=[
            jax.ShapeDtypeStruct((rows, width), BF),
            jax.ShapeDtypeStruct((rows, width * NN), BF),
        ],
        in_specs=[VM] * 2,
        out_specs=[VM] * 2,
        scratch_shapes=[pltpu.VMEM((NN, rows, width), BF), sems, sems, DMA, sems, sems],
        compiler_params=pltpu.CompilerParams(
            collective_id=1, has_side_effects=True, vmem_limit_bytes=LIMIT
        ),
    )(part, cell)


def call_reduce_only(part, base):
    rows, width = base.shape
    sems = DMA((NN - 1,))
    return pl.pallas_call(
        reduce_only,
        name="reduce_only",
        out_shape=jax.ShapeDtypeStruct((rows, width), BF),
        in_specs=[VM] * 2,
        out_specs=VM,
        scratch_shapes=[pltpu.VMEM((NN, rows, width), BF), sems, sems, DMA],
        compiler_params=pltpu.CompilerParams(
            collective_id=2, has_side_effects=True, vmem_limit_bytes=LIMIT
        ),
    )(part, base)


def extended(shard, axis, width):
    size, length = (lax.axis_size(axis), shard.shape[0])
    up = [(i, (i + 1) % size) for i in range(size - 1)]
    down = [(j, i) for i, j in up]
    before = lax.ppermute(shard[length - width :], axis, up)
    after = lax.ppermute(shard[:width], axis, down)
    return jnp.concatenate([before, shard, after], axis=0)


def rms_scale(values, gain):
    mean_square = jnp.mean(values * values, axis=-1, keepdims=True)
    return values * lax.rsqrt(mean_square + epsilon) * gain


def block_mask(layout, query_index):
    wanted = query_index[:, None] + jnp.arange(5, dtype=jnp.int32)[None, :] - 2
    return jnp.any(layout[:, :, None] == wanted[:, None, :], axis=1)


def on_device(cell_rows, attn_gain, ffn_gain, panels, panel_slot, layout):
    row_count = cell_rows.shape[0]
    block_count = row_count // BLK
    cell_full, (attn_panel, up_panel, down_panel) = gather_all(cell_rows, panels[0], panel_slot)
    normed = rms_scale(cell_full.astype(F32), attn_gain).astype(BF)
    projected = jnp.dot(
        normed, attn_panel[:, : 3 * HD], preferred_element_type=F32
    ).astype(BF)
    key_window = extended(projected[:, HD:], "wide", 2 * BLK)
    pair_blocks = key_window.reshape(block_count + 4, BLK, 2, HD)
    stacked = jnp.stack([pair_blocks[o : o + block_count] for o in range(5)], axis=1)
    query_index = (
        lax.axis_index("wide") * block_count
        + jnp.arange(block_count, dtype=jnp.int32)
        + block_count // 2
    ) % NET_BLOCKS
    allowed = block_mask(layout, query_index)
    queries = projected[:, :HD].reshape(block_count, BLK, HD)
    scores = jnp.einsum(
        "bqc,bokc->bqok", queries, stacked[:, :, :, 0, :], preferred_element_type=F32
    ) * HD ** (-0.5)
    lifted = jnp.where(allowed[:, None, :, None], jnp.exp(scores), F32(0.0))
    weights = (lifted / jnp.sum(lifted, axis=(2, 3), keepdims=True)).astype(BF)
    head_out = jnp.einsum(
        "bqok,bokc->bqc", weights, stacked[:, :, :, 1, :], preferred_element_type=F32
    ).astype(BF)
    partial_value = lax.dot_general(
        head_out.reshape(row_count, HD), attn_panel[:, 3 * HD :],
        (((1,), (1,)), ((), ())), preferred_element_type=F32,
    ).astype(BF)
    stream, stream_full = call_reduce_and_gather(partial_value, cell_rows)
    normed_ffn = rms_scale(stream_full.astype(F32), ffn_gain).astype(BF)
    hidden = jax.nn.gelu(
        jnp.dot(normed_ffn, up_panel, preferred_element_type=F32), approximate=False
    ).astype(BF)
    ffn_part = lax.dot_general(
        hidden, down_panel, (((1,), (1,)), ((), ())), preferred_element_type=F32
    ).astype(BF)
    return call_reduce_only(ffn_part, stream)


def solution(mesh):
    return jax.shard_map(
        on_device,
        mesh=mesh,
        in_specs=(P("wide", "narrow"), P(), P(), P("wide", None, "narrow"), P(), P("wide", None)),
        out_specs=P("wide", "narrow"),
        check_vma=False,
    )
```

```python
import functools

import jax
import jax.numpy as jnp
from jax import lax
from jax.experimental import pallas as pl
from jax.experimental.pallas import tpu as pltpu
from jax.sharding import PartitionSpec as P

HD = 128
BLK = 128
NET_BLOCKS = 32
NZ = 16
NW = 64
NN = 8
UP = 8
DOWN = 7
epsilon = 1e-05

BF = jnp.bfloat16
F32 = jnp.float32
VM = pl.BlockSpec(memory_space=pltpu.VMEM)
SM = pl.BlockSpec(memory_space=pltpu.SMEM)
DMA = pltpu.SemaphoreType.DMA
LIMIT = 60 * 1024 * 1024


def remote(src, dst, send, recv, wide, narrow):
    return pltpu.make_async_remote_copy(
        src_ref=src, dst_ref=dst, send_sem=send, recv_sem=recv,
        device_id=(wide, narrow), device_id_type=pl.DeviceIdType.MESH,
    )


def greet(devices):
    barrier = pltpu.get_barrier_semaphore()
    for wide, narrow in devices:
        pl.semaphore_signal(
            barrier, inc=1, device_id=(wide, narrow), device_id_type=pl.DeviceIdType.MESH
        )
    pl.semaphore_wait(barrier, len(devices))


def loop(low, high, body):
    def step(s, carry):
        body(s)
        return carry

    lax.fori_loop(low, high, step, 0)


class Spread:
    def __init__(self, panel, slots, outs, bufs, sems, w, n):
        self.panel, self.slots, self.outs = panel, slots, outs
        self.cbuf, self.rsp, self.rsm, self.ysend, self.yrecv = bufs
        (self.csem, self.psend, self.precv, self.msend, self.mrecv, self.ysem, self.gpsend,
         self.gprecv, self.gmsend, self.gmrecv, self.xsend, self.xrecv) = sems
        self.n, self.core, self.chip = n, w % 2, w // 2
        self.z, self.yl = (w // 2) % NZ, w // (2 * NZ)

        def at_z(zz):
            return (self.yl * NZ + (zz + NZ) % NZ) * 2 + self.core

        self.above, self.below = at_z(self.z + 1), at_z(self.z - 1)
        self.partner = w + 1 - 2 * self.core
        self.across = (w + 2 * NZ) % NW
        self.parts = panel.shape[2]
        self.streams = range(len(outs) * self.parts)
        self.neighbours = [(d, n) for d in (self.partner, self.above, self.below, self.across)]

    def owner(self, i):
        return self.slots[i // self.parts]

    def chip_data(self, i, j):
        part = i % self.parts
        return jnp.where(
            self.owner(i) % 2 == self.core,
            self.panel[j, self.core, part],
            self.cbuf[j, part],
        )

    def here(self, i, mine, other):
        return jnp.where(self.owner(i) // 2 == self.chip, mine, other)

    def up(self, s, i):
        return remote(
            self.rsp.at[s, i], self.rsp.at[s + 1, i],
            self.psend.at[s, i], self.precv.at[s, i], self.above, self.n,
        )

    def down(self, s, i):
        return remote(
            self.rsm.at[s, i], self.rsm.at[s + 1, i],
            self.msend.at[s, i], self.mrecv.at[s, i], self.below, self.n,
        )

    def place(self, chunk, i):
        return self.outs[i // self.parts].at[(chunk + NZ) % NZ, self.core, i % self.parts]

    def gather_up(self, s, i):
        part = self.place(self.z - s, i)
        return remote(part, part, self.gpsend.at[s, i], self.gprecv.at[s, i], self.above, self.n)

    def gather_down(self, s, i):
        part = self.place(self.z + s, i)
        return remote(part, part, self.gmsend.at[s, i], self.gmrecv.at[s, i], self.below, self.n)

    def hand(self, order, chunk, i):
        part = self.place(chunk, i)
        return remote(
            part, part, self.xsend.at[order, i], self.xrecv.at[order, i], self.partner, self.n
        )

    def swap(self, i):
        return remote(
            self.ysend.at[i], self.yrecv.at[i],
            self.ysem.at[0, i], self.ysem.at[1, i], self.across, self.n,
        )

    def to_partner(self):
        return remote(
            self.panel.at[:, 1 - self.core], self.cbuf,
            self.csem.at[0], self.csem.at[1], self.partner, self.n,
        )

    def reduce(self):
        z = self.z
        self.to_partner().wait_recv()
        for i in self.streams:
            self.rsp[0, i] = self.chip_data(i, (z + UP) % NZ)
            self.up(0, i).start()
            self.rsm[0, i] = self.chip_data(i, (z + NZ - DOWN) % NZ)
            self.down(0, i).start()

        def merge_up(s, i):
            self.up(s - 1, i).wait_recv()
            mine = self.chip_data(i, (z + UP - s) % NZ)
            self.rsp[s, i] = self.here(i, mine, self.rsp[s, i])
            self.up(s, i).start()

        def merge_down(s, i):
            self.down(s - 1, i).wait_recv()
            mine = self.chip_data(i, (z + NZ - DOWN + s) % NZ)
            self.rsm[s, i] = self.here(i, mine, self.rsm[s, i])
            self.down(s, i).start()

        def both(s):
            for i in self.streams:
                merge_up(s, i)
                merge_down(s, i)

        loop(1, DOWN, both)
        for i in self.streams:
            merge_up(UP - 1, i)
        for i in self.streams:
            self.up(UP - 1, i).wait_recv()
            self.down(DOWN - 1, i).wait_recv()
            behind = (z - (self.owner(i) // 2) % NZ + NZ) % NZ
            ring = jnp.where(behind <= UP, self.rsp[UP, i], self.rsm[DOWN, i])
            self.ysend[i] = self.here(i, self.chip_data(i, z), ring)
            self.swap(i).start()

    def gather(self):
        z = self.z
        for i in self.streams:
            self.swap(i).wait_recv()
            self.outs[i // self.parts][z, self.core, i % self.parts] = jnp.where(
                self.owner(i) // (2 * NZ) == self.yl, self.ysend[i], self.yrecv[i]
            )
            self.gather_up(0, i).start()
            self.gather_down(0, i).start()
            self.hand(0, z, i).start()

        def relay_up(s, i):
            self.gather_up(s - 1, i).wait_recv()
            self.gather_up(s, i).start()
            self.hand(s, z - s, i).start()

        def relay_down(s, i):
            self.gather_down(s - 1, i).wait_recv()
            self.gather_down(s, i).start()
            self.hand(UP + s, z + s, i).start()

        def relay(s):
            for i in self.streams:
                relay_up(s, i)
                relay_down(s, i)

        loop(1, DOWN, relay)
        for i in self.streams:
            relay_up(DOWN, i)
        for i in self.streams:
            self.gather_up(UP - 1, i).wait_recv()
            self.hand(UP, z - UP, i).start()
            self.gather_down(DOWN - 1, i).wait_recv()
            self.hand(UP + DOWN, z + DOWN, i).start()

    def finish(self):
        self.to_partner().wait_send()

        def sent(s):
            for i in self.streams:
                self.up(s, i).wait_send()
                self.gather_up(s, i).wait_send()

        def sent_down(s):
            for i in self.streams:
                self.down(s, i).wait_send()
                self.gather_down(s, i).wait_send()

        def handed(order):
            for i in self.streams:
                self.hand(order, self.z, i).wait()

        loop(0, UP, sent)
        loop(0, DOWN, sent_down)
        for i in self.streams:
            self.swap(i).wait_send()
        loop(0, NZ, handed)


def spread_scratch(count, parts):
    streams = count * parts
    piece = (64 // parts, 512)
    bufs = [
        pltpu.VMEM((NZ, parts) + piece, BF),
        pltpu.VMEM((UP + 1, streams) + piece, BF),
        pltpu.VMEM((DOWN + 1, streams) + piece, BF),
        pltpu.VMEM((streams,) + piece, BF),
        pltpu.VMEM((streams,) + piece, BF),
    ]
    ups, downs = DMA((UP, streams)), DMA((DOWN, streams))
    sems = [
        DMA((2,)), ups, ups, downs, downs, DMA((2, streams)), ups, ups, downs, downs,
        DMA((NZ, streams)), DMA((NZ, streams)),
    ]
    return bufs + sems


N_BUFS = 5
N_SPREAD = 17


def attn_and_cells(cell, panel, slot, gath, out, *scratch):
    own_sem, nsend, nrecv = scratch[N_SPREAD:]
    w = lax.axis_index("wide")
    n = lax.axis_index("narrow")
    spread = Spread(
        panel, [slot[0]], [out], scratch[:N_BUFS], scratch[N_BUFS:N_SPREAD], w, n
    )
    peers = [(n + k) % NN for k in range(1, NN)]
    greet(spread.neighbours + [(w, p) for p in peers])
    spread.to_partner().start()
    columns = gath.at[:, pl.ds(pl.multiple_of(n * 256, 256), 256)]
    own = pltpu.make_async_copy(cell, columns, own_sem)
    own.start()
    sends = []
    for k in range(1, NN):
        copy = remote(cell, columns, nsend.at[k - 1], nrecv.at[k - 1], w, peers[k - 1])
        copy.start()
        sends.append(copy)
    spread.reduce()
    spread.gather()
    own.wait()
    for copy in sends:
        copy.wait()
    spread.finish()


def call_attn_and_cells(cell_rows, panel, panel_slot):
    rows, width = cell_rows.shape
    parts = 2
    shape = (NZ, 2, parts, 64 // parts, 512)
    gath, out = pl.pallas_call(
        attn_and_cells,
        name="attn_and_cells",
        out_shape=[
            jax.ShapeDtypeStruct((rows, width * NN), BF),
            jax.ShapeDtypeStruct(shape, BF),
        ],
        in_specs=[VM, VM, SM],
        out_specs=[VM] * 2,
        scratch_shapes=spread_scratch(1, parts) + [DMA, DMA((NN - 1,)), DMA((NN - 1,))],
        compiler_params=pltpu.CompilerParams(
            collective_id=0, has_side_effects=True, vmem_limit_bytes=LIMIT
        ),
    )(cell_rows, panel.reshape(shape), panel_slot)
    return gath, out.reshape(2048, 512)


def scatter_rows(part, got, send, recv, own_sem, w, n, peers):
    def columns(p):
        return part.at[:, pl.ds(pl.multiple_of(p * 256, 256), 256)]

    copies = []
    for k in range(1, NN):
        copy = remote(
            columns(peers[k - 1]), got.at[k - 1], send.at[k - 1], recv.at[k - 1], w, peers[k - 1]
        )
        copy.start()
        copies.append(copy)
    own = pltpu.make_async_copy(columns(n), got.at[NN - 1], own_sem)
    own.start()
    return copies + [own]


def summed(base, got, rows):
    total = got[0, rows].astype(F32)
    for k in range(1, NN):
        total = total + got[k, rows].astype(F32)
    return (base[rows].astype(F32) + total).astype(BF)


def reduce_and_gather(part, cell, panel, slot, stream, gath, out0, out1, *scratch):
    got, send, recv, own_sem, send2, recv2 = scratch[N_SPREAD:]
    w = lax.axis_index("wide")
    n = lax.axis_index("narrow")
    spread = Spread(
        panel, [slot[1], slot[2]], [out0, out1],
        scratch[:N_BUFS], scratch[N_BUFS:N_SPREAD], w, n,
    )
    peers = [(n + k) % NN for k in range(1, NN)]
    greet(spread.neighbours + [(w, p) for p in peers])
    spread.to_partner().start()
    parts = scatter_rows(part, got, send, recv, own_sem, w, n, peers)
    spread.reduce()
    for copy in parts:
        copy.wait()

    def block(r):
        rows = pl.ds(pl.multiple_of(r * 64, 64), 64)
        stream[rows] = summed(cell, got, rows)

    loop(0, 8, block)
    columns = gath.at[:, pl.ds(pl.multiple_of(n * 256, 256), 256)]
    own = pltpu.make_async_copy(stream, columns, own_sem)
    own.start()
    copies = []
    for k in range(1, NN):
        copy = remote(stream, columns, send2.at[k - 1], recv2.at[k - 1], w, peers[k - 1])
        copy.start()
        copies.append(copy)
    spread.gather()
    own.wait()
    for copy in copies:
        copy.wait()
    spread.finish()


def reduce_only(part, base, encoded, got, send, recv, own_sem):
    w = lax.axis_index("wide")
    n = lax.axis_index("narrow")
    peers = [(n + k) % NN for k in range(1, NN)]
    greet([(w, p) for p in peers])
    for copy in scatter_rows(part, got, send, recv, own_sem, w, n, peers):
        copy.wait()

    def block(r):
        rows = pl.ds(pl.multiple_of(r * 64, 64), 64)
        encoded[rows] = summed(base, got, rows)

    loop(0, 8, block)


def call_reduce_and_gather(part, cell, panel, panel_slot):
    rows, width = cell.shape
    sems = DMA((NN - 1,))
    parts = 1
    shape = (NZ, 2, parts, 64 // parts, 512)
    stream, gath, *outs = pl.pallas_call(
        reduce_and_gather,
        name="reduce_and_gather",
        out_shape=[
            jax.ShapeDtypeStruct((rows, width), BF),
            jax.ShapeDtypeStruct((rows, width * NN), BF),
            jax.ShapeDtypeStruct(shape, BF),
            jax.ShapeDtypeStruct(shape, BF),
        ],
        in_specs=[VM, VM, VM, SM],
        out_specs=[VM] * 4,
        scratch_shapes=spread_scratch(2, parts)
        + [pltpu.VMEM((NN, rows, width), BF), sems, sems, DMA, sems, sems],
        compiler_params=pltpu.CompilerParams(
            collective_id=1, has_side_effects=True, vmem_limit_bytes=LIMIT
        ),
    )(part, cell, panel.reshape(shape), panel_slot)
    return [stream, gath] + [o.reshape(2048, 512) for o in outs]


def call_reduce_only(part, base):
    rows, width = base.shape
    sems = DMA((NN - 1,))
    return pl.pallas_call(
        reduce_only,
        name="reduce_only",
        out_shape=jax.ShapeDtypeStruct((rows, width), BF),
        in_specs=[VM] * 2,
        out_specs=VM,
        scratch_shapes=[pltpu.VMEM((NN, rows, width), BF), sems, sems, DMA],
        compiler_params=pltpu.CompilerParams(
            collective_id=2, has_side_effects=True, vmem_limit_bytes=LIMIT
        ),
    )(part, base)


def extended(shard, axis, width):
    size, length = (lax.axis_size(axis), shard.shape[0])
    up = [(i, (i + 1) % size) for i in range(size - 1)]
    down = [(j, i) for i, j in up]
    before = lax.ppermute(shard[length - width :], axis, up)
    after = lax.ppermute(shard[:width], axis, down)
    return jnp.concatenate([before, shard, after], axis=0)


def rms_scale(values, gain):
    mean_square = jnp.mean(values * values, axis=-1, keepdims=True)
    return values * lax.rsqrt(mean_square + epsilon) * gain


def block_mask(layout, query_index):
    wanted = query_index[:, None] + jnp.arange(5, dtype=jnp.int32)[None, :] - 2
    return jnp.any(layout[:, :, None] == wanted[:, None, :], axis=1)


def on_device(cell_rows, attn_gain, ffn_gain, panels, panel_slot, layout):
    row_count = cell_rows.shape[0]
    block_count = row_count // BLK
    cell_full, attn_panel = call_attn_and_cells(cell_rows, panels[0], panel_slot)
    normed = rms_scale(cell_full.astype(F32), attn_gain).astype(BF)
    projected = jnp.dot(
        normed, attn_panel[:, : 3 * HD], preferred_element_type=F32
    ).astype(BF)
    key_window = extended(projected[:, HD:], "wide", 2 * BLK)
    pair_blocks = key_window.reshape(block_count + 4, BLK, 2, HD)
    stacked = jnp.stack([pair_blocks[o : o + block_count] for o in range(5)], axis=1)
    query_index = (
        lax.axis_index("wide") * block_count
        + jnp.arange(block_count, dtype=jnp.int32)
        + block_count // 2
    ) % NET_BLOCKS
    allowed = block_mask(layout, query_index)
    queries = projected[:, :HD].reshape(block_count, BLK, HD)
    scores = jnp.einsum(
        "bqc,bokc->bqok", queries, stacked[:, :, :, 0, :], preferred_element_type=F32
    ) * HD ** (-0.5)
    lifted = jnp.where(allowed[:, None, :, None], jnp.exp(scores), F32(0.0))
    weights = (lifted / jnp.sum(lifted, axis=(2, 3), keepdims=True)).astype(BF)
    head_out = jnp.einsum(
        "bqok,bokc->bqc", weights, stacked[:, :, :, 1, :], preferred_element_type=F32
    ).astype(BF)
    partial_value = lax.dot_general(
        head_out.reshape(row_count, HD), attn_panel[:, 3 * HD :],
        (((1,), (1,)), ((), ())), preferred_element_type=F32,
    ).astype(BF)
    stream, stream_full, up_panel, down_panel = call_reduce_and_gather(
        partial_value, cell_rows, panels[0], panel_slot
    )
    normed_ffn = rms_scale(stream_full.astype(F32), ffn_gain).astype(BF)
    hidden = jax.nn.gelu(
        jnp.dot(normed_ffn, up_panel, preferred_element_type=F32), approximate=False
    ).astype(BF)
    ffn_part = lax.dot_general(
        hidden, down_panel, (((1,), (1,)), ((), ())), preferred_element_type=F32
    ).astype(BF)
    return call_reduce_only(ffn_part, stream)


def solution(mesh):
    return jax.shard_map(
        on_device,
        mesh=mesh,
        in_specs=(P("wide", "narrow"), P(), P(), P("wide", None, "narrow"), P(), P("wide", None)),
        out_specs=P("wide", "narrow"),
        check_vma=False,
    )
```

```python
import functools

import jax
import jax.numpy as jnp
from jax import lax
from jax.experimental import pallas as pl
from jax.experimental.pallas import tpu as pltpu
from jax.sharding import PartitionSpec as P

HD = 128
BLK = 128
NET_BLOCKS = 32
NZ = 16
NW = 64
NN = 8
UP = 8
DOWN = 7
epsilon = 1e-05

BF = jnp.bfloat16
F32 = jnp.float32
VM = pl.BlockSpec(memory_space=pltpu.VMEM)
SM = pl.BlockSpec(memory_space=pltpu.SMEM)
DMA = pltpu.SemaphoreType.DMA
LIMIT = 60 * 1024 * 1024


def remote(src, dst, send, recv, wide, narrow):
    return pltpu.make_async_remote_copy(
        src_ref=src, dst_ref=dst, send_sem=send, recv_sem=recv,
        device_id=(wide, narrow), device_id_type=pl.DeviceIdType.MESH,
    )


def greet(devices):
    barrier = pltpu.get_barrier_semaphore()
    for wide, narrow in devices:
        pl.semaphore_signal(
            barrier, inc=1, device_id=(wide, narrow), device_id_type=pl.DeviceIdType.MESH
        )
    pl.semaphore_wait(barrier, len(devices))


def loop(low, high, body):
    def step(s, carry):
        body(s)
        return carry

    lax.fori_loop(low, high, step, 0)


def panels_and_cells(
    cell, panel, slot, gath, out0, out1, out2,
    cbuf, rsp, rsm, ysend, yrecv,
    own_sem, csem, nsend, nrecv, psend, precv, msend, mrecv, ysem,
    gpsend, gprecv, gmsend, gmrecv, xsend, xrecv,
):
    outs = (out0, out1, out2)
    w = lax.axis_index("wide")
    n = lax.axis_index("narrow")
    core = w % 2
    z = (w // 2) % NZ
    yl = w // (2 * NZ)
    chip = w // 2

    def at_z(zz):
        return (yl * NZ + (zz + NZ) % NZ) * 2 + core

    above, below = at_z(z + 1), at_z(z - 1)
    partner = w + 1 - 2 * core
    across = (w + 2 * NZ) % NW
    peers = [(n + k) % NN for k in range(1, NN)]
    greet(
        [(partner, n), (above, n), (below, n), (across, n)] + [(w, p) for p in peers]
    )
    to_partner = remote(panel.at[:, 1 - core], cbuf, csem.at[0], csem.at[1], partner, n)
    to_partner.start()
    columns = gath.at[:, pl.ds(pl.multiple_of(n * 256, 256), 256)]
    own = pltpu.make_async_copy(cell, columns, own_sem)
    own.start()
    sends = []
    for k in range(1, NN):
        copy = remote(cell, columns, nsend.at[k - 1], nrecv.at[k - 1], w, peers[k - 1])
        copy.start()
        sends.append(copy)
    to_partner.wait_recv()

    slots = [slot[i] for i in range(3)]

    def chip_data(i, j):
        return jnp.where(slots[i] % 2 == core, panel[j, core], cbuf[j])

    def up(s, i):
        return remote(rsp.at[s, i], rsp.at[s + 1, i], psend.at[s, i], precv.at[s, i], above, n)

    def down(s, i):
        return remote(rsm.at[s, i], rsm.at[s + 1, i], msend.at[s, i], mrecv.at[s, i], below, n)

    for i in range(3):
        rsp[0, i] = chip_data(i, (z + UP) % NZ)
        up(0, i).start()
        rsm[0, i] = chip_data(i, (z + NZ - DOWN) % NZ)
        down(0, i).start()

    def merge_up(s, i):
        up(s - 1, i).wait_recv()
        mine = chip_data(i, (z + UP - s) % NZ)
        rsp[s, i] = jnp.where(slots[i] // 2 == chip, mine, rsp[s, i])
        up(s, i).start()

    def merge_down(s, i):
        down(s - 1, i).wait_recv()
        mine = chip_data(i, (z + NZ - DOWN + s) % NZ)
        rsm[s, i] = jnp.where(slots[i] // 2 == chip, mine, rsm[s, i])
        down(s, i).start()

    def both(s):
        for i in range(3):
            merge_up(s, i)
            merge_down(s, i)

    loop(1, DOWN, both)
    for i in range(3):
        merge_up(UP - 1, i)

    def swap(i):
        return remote(ysend.at[i], yrecv.at[i], ysem.at[0, i], ysem.at[1, i], across, n)

    for i in range(3):
        up(UP - 1, i).wait_recv()
        down(DOWN - 1, i).wait_recv()
        behind = (z - (slots[i] // 2) % NZ + NZ) % NZ
        ring = jnp.where(behind <= UP, rsp[UP, i], rsm[DOWN, i])
        ysend[i] = jnp.where(slots[i] // 2 == chip, chip_data(i, z), ring)
        swap(i).start()

    def gather_up(s, i):
        part = outs[i].at[(z - s + NZ) % NZ, core]
        return remote(part, part, gpsend.at[s, i], gprecv.at[s, i], above, n)

    def gather_down(s, i):
        part = outs[i].at[(z + s) % NZ, core]
        return remote(part, part, gmsend.at[s, i], gmrecv.at[s, i], below, n)

    def hand(order, chunk, i):
        part = outs[i].at[(chunk + NZ) % NZ, core]
        return remote(part, part, xsend.at[order, i], xrecv.at[order, i], partner, n)

    for i in range(3):
        swap(i).wait_recv()
        outs[i][z, core] = jnp.where(slots[i] // (2 * NZ) == yl, ysend[i], yrecv[i])
        gather_up(0, i).start()
        gather_down(0, i).start()
        hand(0, z, i).start()

    def relay_up(s, i):
        gather_up(s - 1, i).wait_recv()
        gather_up(s, i).start()
        hand(s, z - s, i).start()

    def relay_down(s, i):
        gather_down(s - 1, i).wait_recv()
        gather_down(s, i).start()
        hand(UP + s, z + s, i).start()

    def relay(s):
        for i in range(3):
            relay_up(s, i)
            relay_down(s, i)

    loop(1, DOWN, relay)
    for i in range(3):
        relay_up(DOWN, i)
    for i in range(3):
        gather_up(UP - 1, i).wait_recv()
        hand(UP, z - UP, i).start()
        gather_down(DOWN - 1, i).wait_recv()
        hand(UP + DOWN, z + DOWN, i).start()

    own.wait()
    to_partner.wait_send()
    for copy in sends:
        copy.wait()

    def finish(s):
        for i in range(3):
            up(s, i).wait_send()
            gather_up(s, i).wait_send()

            @pl.when(s < DOWN)
            def _():
                down(s, i).wait_send()
                gather_down(s, i).wait_send()

    loop(0, UP, finish)
    for i in range(3):
        swap(i).wait_send()

    def handed(order):
        for i in range(3):
            hand(order, z, i).wait()

    loop(0, NZ, handed)


def gather_all(cell_rows, panel, panel_slot):
    rows, width = cell_rows.shape
    piece = (64, 512)
    big = jax.ShapeDtypeStruct((NZ, 2, 64, 512), BF)
    gath, *outs = pl.pallas_call(
        panels_and_cells,
        name="panels_and_cells",
        out_shape=[jax.ShapeDtypeStruct((rows, width * NN), BF), big, big, big],
        in_specs=[VM, VM, SM],
        out_specs=[VM] * 4,
        scratch_shapes=[
            pltpu.VMEM((NZ,) + piece, BF),
            pltpu.VMEM((UP + 1, 3) + piece, BF),
            pltpu.VMEM((DOWN + 1, 3) + piece, BF),
            pltpu.VMEM((3,) + piece, BF),
            pltpu.VMEM((3,) + piece, BF),
            DMA, DMA((2,)), DMA((NN - 1,)), DMA((NN - 1,)),
            DMA((UP, 3)), DMA((UP, 3)), DMA((DOWN, 3)), DMA((DOWN, 3)), DMA((2, 3)),
            DMA((UP, 3)), DMA((UP, 3)), DMA((DOWN, 3)), DMA((DOWN, 3)),
            DMA((NZ, 3)), DMA((NZ, 3)),
        ],
        compiler_params=pltpu.CompilerParams(
            collective_id=0, has_side_effects=True, vmem_limit_bytes=LIMIT
        ),
    )(cell_rows, panel.reshape((NZ, 2, 64, 512)), panel_slot)
    return gath, [o.reshape(2048, 512) for o in outs]


class Narrow:
    def __init__(self):
        self.w, self.n = lax.axis_index("wide"), lax.axis_index("narrow")
        self.x, self.h = self.n // 2, self.n % 2
        self.right = (self.w, (self.n + 2) % NN)
        self.left = (self.w, (self.n + NN - 2) % NN)
        self.pair = (self.w, self.n + 1 - 2 * self.h)
        self.devices = [self.right, self.left, self.pair]


CH = 4
ROWS = 512 // CH


def rows_of(c):
    return pl.ds(c * ROWS, ROWS)


class Sum:
    def __init__(self, net, part, bufs, sems):
        self.net, self.part = net, part
        self.far, self.relay, self.near_r, self.near_l, self.ysend, self.yrecv = bufs
        self.fs, self.fr, self.rs, self.rr, self.ls, self.lr, self.ys, self.yr = sems

    def block(self, x, c):
        start = pl.multiple_of(((x + 4) % 4) * 512, 512)
        return self.part.at[rows_of(c), pl.ds(start, 512)]

    def to_far(self, c):
        target = self.net.right if c % 2 == 0 else self.net.left
        return remote(
            self.block(self.net.x + 2, c), self.far.at[c], self.fs.at[c], self.fr.at[c], *target
        )

    def to_right(self, c):
        source = self.relay.at[c] if c % 2 == 0 else self.block(self.net.x + 1, c)
        return remote(source, self.near_r.at[c], self.rs.at[c], self.rr.at[c], *self.net.right)

    def to_left(self, c):
        source = self.relay.at[c] if c % 2 == 1 else self.block(self.net.x - 1, c)
        return remote(source, self.near_l.at[c], self.ls.at[c], self.lr.at[c], *self.net.left)

    def to_pair(self, c):
        return remote(
            self.ysend.at[c], self.yrecv.at[c], self.ys.at[c], self.yr.at[c], *self.net.pair
        )

    def start(self):
        for c in range(CH):
            self.to_far(c).start()

    def forward(self, c):
        self.to_far(c).wait_recv()
        step = 1 if c % 2 == 0 else -1
        mine = self.block(self.net.x + step, c)[...]
        self.relay[c] = (mine.astype(F32) + self.far[c].astype(F32)).astype(BF)
        self.to_right(c).start()
        self.to_left(c).start()

    def columns(self, c, h):
        start = pl.multiple_of((self.net.x * 2 + h) * 256, 256)
        cols = pl.ds(pl.multiple_of(h * 256, 256), 256)
        total = self.part[rows_of(c), pl.ds(start, 256)].astype(F32)
        total = total + self.near_r[c, :, cols].astype(F32)
        return total + self.near_l[c, :, cols].astype(F32)

    def cross(self, c):
        self.to_right(c).wait_recv()
        self.to_left(c).wait_recv()
        self.ysend[c] = self.columns(c, 1 - self.net.h).astype(BF)
        self.to_pair(c).start()

    def total(self, c):
        self.to_pair(c).wait_recv()
        return self.columns(c, self.net.h) + self.yrecv[c].astype(F32)

    def finish(self):
        for c in range(CH):
            self.to_far(c).wait_send()
            self.to_right(c).wait_send()
            self.to_left(c).wait_send()
            self.to_pair(c).wait_send()


SUM_SCRATCH = (
    [pltpu.VMEM((CH, ROWS, 512), BF)] * 4
    + [pltpu.VMEM((CH, ROWS, 256), BF)] * 2
    + [DMA((CH,))] * 8
)


class Gather:
    def __init__(self, net, piece, gath, sems):
        self.net, self.piece, self.gath = net, piece, gath
        self.ys, self.yr, self.rs, self.rr, self.ls, self.lr, self.fs, self.fr = sems

    def place(self, x, q, c):
        h = self.net.h if q == 0 else 1 - self.net.h
        start = pl.multiple_of((((x + 4) % 4) * 2 + h) * 256, 256)
        return self.gath.at[rows_of(c), pl.ds(start, 256)]

    def source(self, q, c):
        return self.piece.at[rows_of(c)] if q == 0 else self.place(self.net.x, 1, c)

    def to_pair(self, c):
        return remote(
            self.source(0, c), self.place(self.net.x, 0, c),
            self.ys.at[c], self.yr.at[c], *self.net.pair,
        )

    def to_right(self, q, c):
        return remote(
            self.source(q, c), self.place(self.net.x, q, c),
            self.rs.at[q, c], self.rr.at[q, c], *self.net.right,
        )

    def to_left(self, q, c):
        return remote(
            self.source(q, c), self.place(self.net.x, q, c),
            self.ls.at[q, c], self.lr.at[q, c], *self.net.left,
        )

    def onward(self, q, c):
        step, target = (-1, self.net.right) if c % 2 == 0 else (1, self.net.left)
        part = self.place(self.net.x + step, q, c)
        return remote(part, part, self.fs.at[q, c], self.fr.at[q, c], *target)

    def start(self, c):
        self.to_pair(c).start()
        self.to_right(0, c).start()
        self.to_left(0, c).start()

    def spread_pair(self, c):
        self.to_pair(c).wait_recv()
        self.to_right(1, c).start()
        self.to_left(1, c).start()

    def relay(self, q, c):
        self.to_right(q, c).wait_recv()
        self.to_left(q, c).wait_recv()
        self.onward(q, c).start()

    def finish(self):
        for c in range(CH):
            self.to_pair(c).wait_send()
            for q in range(2):
                self.to_right(q, c).wait_send()
                self.to_left(q, c).wait_send()
                self.onward(q, c).wait()


GATHER_SCRATCH = [DMA((CH,))] * 2 + [DMA((2, CH))] * 6


def reduce_and_gather(part, cell, stream, gath, own_sem, *scratch):
    net = Narrow()
    greet(net.devices)
    add = Sum(net, part, scratch[:6], scratch[6:14])
    spread = Gather(net, stream, gath, scratch[14:])
    add.start()
    for c in range(CH):
        add.forward(c)
    for c in range(CH):
        add.cross(c)
    columns = gath.at[:, pl.ds(pl.multiple_of(net.n * 256, 256), 256)]
    for c in range(CH):
        total = cell[rows_of(c)].astype(F32) + add.total(c)
        stream[rows_of(c)] = total.astype(BF)
        spread.start(c)
    own = pltpu.make_async_copy(stream, columns, own_sem)
    own.start()
    for c in range(CH):
        spread.spread_pair(c)
    for q in range(2):
        for c in range(CH):
            spread.relay(q, c)
    own.wait()
    add.finish()
    spread.finish()


def reduce_only(part, base, encoded, *scratch):
    net = Narrow()
    greet(net.devices)
    add = Sum(net, part, scratch[:6], scratch[6:])
    add.start()
    for c in range(CH):
        add.forward(c)
    for c in range(CH):
        add.cross(c)
    for c in range(CH):
        total = base[rows_of(c)].astype(F32) + add.total(c)
        encoded[rows_of(c)] = total.astype(BF)
    add.finish()


def call_reduce_and_gather(part, cell):
    rows, width = cell.shape
    return pl.pallas_call(
        reduce_and_gather,
        name="reduce_and_gather",
        out_shape=[
            jax.ShapeDtypeStruct((rows, width), BF),
            jax.ShapeDtypeStruct((rows, width * NN), BF),
        ],
        in_specs=[VM] * 2,
        out_specs=[VM] * 2,
        scratch_shapes=[DMA] + SUM_SCRATCH + GATHER_SCRATCH,
        compiler_params=pltpu.CompilerParams(
            collective_id=1, has_side_effects=True, vmem_limit_bytes=LIMIT
        ),
    )(part, cell)


def call_reduce_only(part, base):
    rows, width = base.shape
    return pl.pallas_call(
        reduce_only,
        name="reduce_only",
        out_shape=jax.ShapeDtypeStruct((rows, width), BF),
        in_specs=[VM] * 2,
        out_specs=VM,
        scratch_shapes=SUM_SCRATCH,
        compiler_params=pltpu.CompilerParams(
            collective_id=2, has_side_effects=True, vmem_limit_bytes=LIMIT
        ),
    )(part, base)


def extended(shard, axis, width):
    size, length = (lax.axis_size(axis), shard.shape[0])
    up = [(i, (i + 1) % size) for i in range(size - 1)]
    down = [(j, i) for i, j in up]
    before = lax.ppermute(shard[length - width :], axis, up)
    after = lax.ppermute(shard[:width], axis, down)
    return jnp.concatenate([before, shard, after], axis=0)


def rms_scale(values, gain):
    mean_square = jnp.mean(values * values, axis=-1, keepdims=True)
    return values * lax.rsqrt(mean_square + epsilon) * gain


def block_mask(layout, query_index):
    wanted = query_index[:, None] + jnp.arange(5, dtype=jnp.int32)[None, :] - 2
    return jnp.any(layout[:, :, None] == wanted[:, None, :], axis=1)


def on_device(cell_rows, attn_gain, ffn_gain, panels, panel_slot, layout):
    row_count = cell_rows.shape[0]
    block_count = row_count // BLK
    cell_full, (attn_panel, up_panel, down_panel) = gather_all(cell_rows, panels[0], panel_slot)
    normed = rms_scale(cell_full.astype(F32), attn_gain).astype(BF)
    projected = jnp.dot(
        normed, attn_panel[:, : 3 * HD], preferred_element_type=F32
    ).astype(BF)
    key_window = extended(projected[:, HD:], "wide", 2 * BLK)
    pair_blocks = key_window.reshape(block_count + 4, BLK, 2, HD)
    stacked = jnp.stack([pair_blocks[o : o + block_count] for o in range(5)], axis=1)
    query_index = (
        lax.axis_index("wide") * block_count
        + jnp.arange(block_count, dtype=jnp.int32)
        + block_count // 2
    ) % NET_BLOCKS
    allowed = block_mask(layout, query_index)
    queries = projected[:, :HD].reshape(block_count, BLK, HD)
    scores = jnp.einsum(
        "bqc,bokc->bqok", queries, stacked[:, :, :, 0, :], preferred_element_type=F32
    ) * HD ** (-0.5)
    lifted = jnp.where(allowed[:, None, :, None], jnp.exp(scores), F32(0.0))
    weights = (lifted / jnp.sum(lifted, axis=(2, 3), keepdims=True)).astype(BF)
    head_out = jnp.einsum(
        "bqok,bokc->bqc", weights, stacked[:, :, :, 1, :], preferred_element_type=F32
    ).astype(BF)
    partial_value = lax.dot_general(
        head_out.reshape(row_count, HD), attn_panel[:, 3 * HD :],
        (((1,), (1,)), ((), ())), preferred_element_type=F32,
    ).astype(BF)
    stream, stream_full = call_reduce_and_gather(partial_value, cell_rows)
    normed_ffn = rms_scale(stream_full.astype(F32), ffn_gain).astype(BF)
    hidden = jax.nn.gelu(
        jnp.dot(normed_ffn, up_panel, preferred_element_type=F32), approximate=False
    ).astype(BF)
    ffn_part = lax.dot_general(
        hidden, down_panel, (((1,), (1,)), ((), ())), preferred_element_type=F32
    ).astype(BF)
    return call_reduce_only(ffn_part, stream)


def solution(mesh):
    return jax.shard_map(
        on_device,
        mesh=mesh,
        in_specs=(P("wide", "narrow"), P(), P(), P("wide", None, "narrow"), P(), P("wide", None)),
        out_specs=P("wide", "narrow"),
        check_vma=False,
    )
```

```python
import functools

import jax
import jax.numpy as jnp
from jax import lax
from jax.experimental import pallas as pl
from jax.experimental.pallas import tpu as pltpu
from jax.sharding import PartitionSpec as P

HD = 128
BLK = 128
NET_BLOCKS = 32
NZ = 16
NW = 64
NN = 8
UP = 8
DOWN = 7
epsilon = 1e-05

BF = jnp.bfloat16
F32 = jnp.float32
VM = pl.BlockSpec(memory_space=pltpu.VMEM)
SM = pl.BlockSpec(memory_space=pltpu.SMEM)
DMA = pltpu.SemaphoreType.DMA
LIMIT = 60 * 1024 * 1024


def remote(src, dst, send, recv, wide, narrow):
    return pltpu.make_async_remote_copy(
        src_ref=src, dst_ref=dst, send_sem=send, recv_sem=recv,
        device_id=(wide, narrow), device_id_type=pl.DeviceIdType.MESH,
    )


def greet(devices):
    barrier = pltpu.get_barrier_semaphore()
    for wide, narrow in devices:
        pl.semaphore_signal(
            barrier, inc=1, device_id=(wide, narrow), device_id_type=pl.DeviceIdType.MESH
        )
    pl.semaphore_wait(barrier, len(devices))


def loop(low, high, body):
    def step(s, carry):
        body(s)
        return carry

    lax.fori_loop(low, high, step, 0)


class Place:
    def __init__(self):
        self.w, self.n = lax.axis_index("wide"), lax.axis_index("narrow")
        self.core, self.chip = self.w % 2, self.w // 2
        self.z, self.yl = self.chip % NZ, self.w // (2 * NZ)
        self.above = (self.at_z(self.z + 1), self.n)
        self.below = (self.at_z(self.z - 1), self.n)
        self.partner = (self.w + 1 - 2 * self.core, self.n)
        self.across = ((self.w + 2 * NZ) % NW, self.n)

    def at_z(self, zz):
        return (self.yl * NZ + (zz + NZ) % NZ) * 2 + self.core


class Pick:
    def __init__(self, at, panel, slots, bufs, sems):
        self.at, self.panel, self.slots = at, panel, slots
        self.cbuf, self.rsp, self.rsm, self.ysend, self.yrecv = bufs
        self.csem, self.psend, self.precv, self.msend, self.mrecv, self.ysem = sems
        self.parts = panel.shape[2]
        self.count = len(slots) * self.parts

    def owner(self, i):
        return self.slots[i // self.parts]

    def chip_data(self, i, j):
        part = i % self.parts
        return jnp.where(
            self.owner(i) % 2 == self.at.core,
            self.panel[j, self.at.core, part],
            self.cbuf[j, part],
        )

    def here(self, i, mine, other):
        return jnp.where(self.owner(i) // 2 == self.at.chip, mine, other)

    def up(self, s, i):
        return remote(
            self.rsp.at[s, i], self.rsp.at[s + 1, i],
            self.psend.at[s, i], self.precv.at[s, i], *self.at.above,
        )

    def down(self, s, i):
        return remote(
            self.rsm.at[s, i], self.rsm.at[s + 1, i],
            self.msend.at[s, i], self.mrecv.at[s, i], *self.at.below,
        )

    def swap(self, i):
        return remote(
            self.ysend.at[i], self.yrecv.at[i],
            self.ysem.at[0, i], self.ysem.at[1, i], *self.at.across,
        )

    def to_partner(self):
        return remote(
            self.panel.at[:, 1 - self.at.core], self.cbuf,
            self.csem.at[0], self.csem.at[1], *self.at.partner,
        )

    def begin(self, i):
        self.rsp[0, i] = self.chip_data(i, (self.at.z + UP) % NZ)
        self.up(0, i).start()
        self.rsm[0, i] = self.chip_data(i, (self.at.z + NZ - DOWN) % NZ)
        self.down(0, i).start()

    def merge_up(self, s, i):
        self.up(s - 1, i).wait_recv()
        mine = self.chip_data(i, (self.at.z + UP - s) % NZ)
        self.rsp[s, i] = self.here(i, mine, self.rsp[s, i])
        self.up(s, i).start()

    def merge_down(self, s, i):
        self.down(s - 1, i).wait_recv()
        mine = self.chip_data(i, (self.at.z + NZ - DOWN + s) % NZ)
        self.rsm[s, i] = self.here(i, mine, self.rsm[s, i])
        self.down(s, i).start()

    def end(self, i):
        self.up(UP - 1, i).wait_recv()
        self.down(DOWN - 1, i).wait_recv()
        behind = (self.at.z - (self.owner(i) // 2) % NZ + NZ) % NZ
        ring = jnp.where(behind <= UP, self.rsp[UP, i], self.rsm[DOWN, i])
        self.ysend[i] = self.here(i, self.chip_data(i, self.at.z), ring)
        self.swap(i).start()

    def result(self, i):
        self.swap(i).wait_recv()
        return jnp.where(
            self.owner(i) // (2 * NZ) == self.at.yl, self.ysend[i], self.yrecv[i]
        )

    def finish(self):
        self.to_partner().wait_send()

        def sent(s):
            for i in range(self.count):
                self.up(s, i).wait_send()

        def sent_down(s):
            for i in range(self.count):
                self.down(s, i).wait_send()

        loop(0, UP, sent)
        loop(0, DOWN, sent_down)
        for i in range(self.count):
            self.swap(i).wait_send()


class Fan:
    def __init__(self, at, outs, sems):
        self.at, self.outs = at, outs
        self.gpsend, self.gprecv, self.gmsend, self.gmrecv, self.xsend, self.xrecv = sems
        self.parts = outs[0].shape[2]
        self.streams = range(len(outs) * self.parts)

    def place(self, chunk, i):
        return self.outs[i // self.parts].at[(chunk + NZ) % NZ, self.at.core, i % self.parts]

    def up(self, s, i, source=None):
        part = self.place(self.at.z - s, i)
        source = part if source is None else source
        return remote(source, part, self.gpsend.at[s, i], self.gprecv.at[s, i], *self.at.above)

    def down(self, s, i, source=None):
        part = self.place(self.at.z + s, i)
        source = part if source is None else source
        return remote(source, part, self.gmsend.at[s, i], self.gmrecv.at[s, i], *self.at.below)

    def hand(self, order, chunk, i, source=None):
        part = self.place(chunk, i)
        source = part if source is None else source
        return remote(
            source, part, self.xsend.at[order, i], self.xrecv.at[order, i], *self.at.partner
        )

    def begin(self, i, source=None):
        self.up(0, i, source).start()
        self.down(0, i, source).start()
        self.hand(0, self.at.z, i, source).start()

    def relay_up(self, s, i):
        self.up(s - 1, i).wait_recv()
        self.up(s, i).start()
        self.hand(s, self.at.z - s, i).start()

    def relay_down(self, s, i):
        self.down(s - 1, i).wait_recv()
        self.down(s, i).start()
        self.hand(UP + s, self.at.z + s, i).start()

    def relay(self, s):
        for i in self.streams:
            self.relay_up(s, i)
            self.relay_down(s, i)

    def last(self):
        for i in self.streams:
            self.relay_up(DOWN, i)

    def end(self):
        for i in self.streams:
            self.up(UP - 1, i).wait_recv()
            self.hand(UP, self.at.z - UP, i).start()
            self.down(DOWN - 1, i).wait_recv()
            self.hand(UP + DOWN, self.at.z + DOWN, i).start()

    def finish(self):
        def sent(s):
            for i in self.streams:
                self.up(s, i).wait_send()

        def sent_down(s):
            for i in self.streams:
                self.down(s, i).wait_send()

        def handed(order):
            for i in self.streams:
                self.hand(order, self.at.z, i).wait()

        loop(0, UP, sent)
        loop(0, DOWN, sent_down)
        loop(0, NZ, handed)


PARTS = 2


def pick_scratch():
    piece = (64 // PARTS, 512)
    count = 3 * PARTS
    ups, downs = DMA((UP, count)), DMA((DOWN, count))
    return [
        pltpu.VMEM((NZ, PARTS) + piece, BF),
        pltpu.VMEM((UP + 1, count) + piece, BF),
        pltpu.VMEM((DOWN + 1, count) + piece, BF),
        pltpu.VMEM((count,) + piece, BF),
        pltpu.VMEM((count,) + piece, BF),
        DMA((2,)), ups, ups, downs, downs, DMA((2, count)),
    ]


def fan_scratch(count):
    ups, downs, hands = DMA((UP, count)), DMA((DOWN, count)), DMA((NZ, count))
    return [ups, ups, downs, downs, hands, hands]


def panels_and_cells(cell, panel, slot, gath, out, shares, *scratch):
    at = Place()
    pick = Pick(at, panel, [slot[i] for i in range(3)], scratch[:5], scratch[5:11])
    fan = Fan(at, [out], scratch[11:17])
    own_sem, nsend, nrecv = scratch[17:]
    w, n = at.w, at.n
    peers = [(n + k) % NN for k in range(1, NN)]
    greet([at.partner, at.above, at.below, at.across] + [(w, p) for p in peers])
    pick.to_partner().start()
    columns = gath.at[:, pl.ds(pl.multiple_of(n * 256, 256), 256)]
    own = pltpu.make_async_copy(cell, columns, own_sem)
    own.start()
    sends = []
    for k in range(1, NN):
        copy = remote(cell, columns, nsend.at[k - 1], nrecv.at[k - 1], w, peers[k - 1])
        copy.start()
        sends.append(copy)
    first = range(2 * PARTS)
    later = range(2 * PARTS, 3 * PARTS)
    pick.to_partner().wait_recv()
    for i in first:
        pick.begin(i)

    def both(s):
        for i in first:
            pick.merge_up(s, i)
            pick.merge_down(s, i)

    loop(1, DOWN, both)
    for i in first:
        pick.merge_up(UP - 1, i)
    for i in first:
        pick.end(i)
    for i in range(PARTS):
        out[at.z, at.core, i] = pick.result(i)
        fan.begin(i)
    for i in later:
        pick.begin(i)

    def mixed(s):
        fan.relay(s)
        for i in later:
            pick.merge_up(s, i)
            pick.merge_down(s, i)

    loop(1, DOWN, mixed)
    fan.last()
    for i in later:
        pick.merge_up(UP - 1, i)
    fan.end()
    for i in later:
        pick.end(i)
    for i in range(PARTS, 3 * PARTS):
        shares[i - PARTS] = pick.result(i)
    own.wait()
    for copy in sends:
        copy.wait()
    pick.finish()
    fan.finish()


def gather_all(cell_rows, panel, panel_slot):
    rows, width = cell_rows.shape
    shape = (NZ, 2, PARTS, 64 // PARTS, 512)
    gath, out, shares = pl.pallas_call(
        panels_and_cells,
        name="panels_and_cells",
        out_shape=[
            jax.ShapeDtypeStruct((rows, width * NN), BF),
            jax.ShapeDtypeStruct(shape, BF),
            jax.ShapeDtypeStruct((2 * PARTS, 64 // PARTS, 512), BF),
        ],
        in_specs=[VM, VM, SM],
        out_specs=[VM] * 3,
        scratch_shapes=pick_scratch()
        + fan_scratch(PARTS)
        + [DMA, DMA((NN - 1,)), DMA((NN - 1,))],
        compiler_params=pltpu.CompilerParams(
            collective_id=0, has_side_effects=True, vmem_limit_bytes=LIMIT
        ),
    )(cell_rows, panel.reshape(shape), panel_slot)
    return gath, out.reshape(2048, 512), shares.reshape(2, 64, 512)


class Narrow:
    def __init__(self):
        self.w, self.n = lax.axis_index("wide"), lax.axis_index("narrow")
        self.x, self.h = self.n // 2, self.n % 2
        self.right = (self.w, (self.n + 2) % NN)
        self.left = (self.w, (self.n + NN - 2) % NN)
        self.pair = (self.w, self.n + 1 - 2 * self.h)
        self.devices = [self.right, self.left, self.pair]


CH = 4
ROWS = 512 // CH


def rows_of(c):
    return pl.ds(c * ROWS, ROWS)


class Sum:
    def __init__(self, net, part, bufs, sems):
        self.net, self.part = net, part
        self.far, self.relay, self.near_r, self.near_l, self.ysend, self.yrecv = bufs
        self.fs, self.fr, self.rs, self.rr, self.ls, self.lr, self.ys, self.yr = sems

    def block(self, x, c):
        start = pl.multiple_of(((x + 4) % 4) * 512, 512)
        return self.part.at[rows_of(c), pl.ds(start, 512)]

    def to_far(self, c):
        target = self.net.right if c % 2 == 0 else self.net.left
        return remote(
            self.block(self.net.x + 2, c), self.far.at[c], self.fs.at[c], self.fr.at[c], *target
        )

    def to_right(self, c):
        source = self.relay.at[c] if c % 2 == 0 else self.block(self.net.x + 1, c)
        return remote(source, self.near_r.at[c], self.rs.at[c], self.rr.at[c], *self.net.right)

    def to_left(self, c):
        source = self.relay.at[c] if c % 2 == 1 else self.block(self.net.x - 1, c)
        return remote(source, self.near_l.at[c], self.ls.at[c], self.lr.at[c], *self.net.left)

    def to_pair(self, c):
        return remote(
            self.ysend.at[c], self.yrecv.at[c], self.ys.at[c], self.yr.at[c], *self.net.pair
        )

    def start(self):
        for c in range(CH):
            self.to_far(c).start()

    def forward(self, c):
        self.to_far(c).wait_recv()
        step = 1 if c % 2 == 0 else -1
        mine = self.block(self.net.x + step, c)[...]
        self.relay[c] = (mine.astype(F32) + self.far[c].astype(F32)).astype(BF)
        self.to_right(c).start()
        self.to_left(c).start()

    def columns(self, c, h):
        start = pl.multiple_of((self.net.x * 2 + h) * 256, 256)
        cols = pl.ds(pl.multiple_of(h * 256, 256), 256)
        total = self.part[rows_of(c), pl.ds(start, 256)].astype(F32)
        total = total + self.near_r[c, :, cols].astype(F32)
        return total + self.near_l[c, :, cols].astype(F32)

    def cross(self, c):
        self.to_right(c).wait_recv()
        self.to_left(c).wait_recv()
        self.ysend[c] = self.columns(c, 1 - self.net.h).astype(BF)
        self.to_pair(c).start()

    def total(self, c):
        self.to_pair(c).wait_recv()
        return self.columns(c, self.net.h) + self.yrecv[c].astype(F32)

    def finish(self):
        for c in range(CH):
            self.to_far(c).wait_send()
            self.to_right(c).wait_send()
            self.to_left(c).wait_send()
            self.to_pair(c).wait_send()


SUM_SCRATCH = (
    [pltpu.VMEM((CH, ROWS, 512), BF)] * 4
    + [pltpu.VMEM((CH, ROWS, 256), BF)] * 2
    + [DMA((CH,))] * 8
)


class Gather:
    def __init__(self, net, piece, gath, sems):
        self.net, self.piece, self.gath = net, piece, gath
        self.ys, self.yr, self.rs, self.rr, self.ls, self.lr, self.fs, self.fr = sems

    def place(self, x, q, c):
        h = self.net.h if q == 0 else 1 - self.net.h
        start = pl.multiple_of((((x + 4) % 4) * 2 + h) * 256, 256)
        return self.gath.at[rows_of(c), pl.ds(start, 256)]

    def source(self, q, c):
        return self.piece.at[rows_of(c)] if q == 0 else self.place(self.net.x, 1, c)

    def to_pair(self, c):
        return remote(
            self.source(0, c), self.place(self.net.x, 0, c),
            self.ys.at[c], self.yr.at[c], *self.net.pair,
        )

    def to_right(self, q, c):
        return remote(
            self.source(q, c), self.place(self.net.x, q, c),
            self.rs.at[q, c], self.rr.at[q, c], *self.net.right,
        )

    def to_left(self, q, c):
        return remote(
            self.source(q, c), self.place(self.net.x, q, c),
            self.ls.at[q, c], self.lr.at[q, c], *self.net.left,
        )

    def onward(self, q, c):
        step, target = (-1, self.net.right) if c % 2 == 0 else (1, self.net.left)
        part = self.place(self.net.x + step, q, c)
        return remote(part, part, self.fs.at[q, c], self.fr.at[q, c], *target)

    def start(self, c):
        self.to_pair(c).start()
        self.to_right(0, c).start()
        self.to_left(0, c).start()

    def spread_pair(self, c):
        self.to_pair(c).wait_recv()
        self.to_right(1, c).start()
        self.to_left(1, c).start()

    def relay(self, q, c):
        self.to_right(q, c).wait_recv()
        self.to_left(q, c).wait_recv()
        self.onward(q, c).start()

    def finish(self):
        for c in range(CH):
            self.to_pair(c).wait_send()
            for q in range(2):
                self.to_right(q, c).wait_send()
                self.to_left(q, c).wait_send()
                self.onward(q, c).wait()


GATHER_SCRATCH = [DMA((CH,))] * 2 + [DMA((2, CH))] * 6


def reduce_and_gather(part, cell, shares, stream, gath, out0, out1, own_sem, share_sem, *scratch):
    net = Narrow()
    at = Place()
    greet(net.devices + [at.partner, at.above, at.below])
    add = Sum(net, part, scratch[:6], scratch[6:14])
    spread = Gather(net, stream, gath, scratch[14:22])
    fan = Fan(at, [out0, out1], scratch[22:])
    add.start()
    kept = []
    for i in fan.streams:
        fan.begin(i, shares.at[i])
        copy = pltpu.make_async_copy(shares.at[i], fan.place(at.z, i), share_sem.at[i])
        copy.start()
        kept.append(copy)
    for c in range(CH):
        add.forward(c)
        if c % 2 == 1:
            fan.relay(c // 2 + 1)
    for c in range(CH):
        add.cross(c)
        if c % 2 == 1:
            fan.relay(c // 2 + 3)
    columns = gath.at[:, pl.ds(pl.multiple_of(net.n * 256, 256), 256)]
    for c in range(CH):
        total = cell[rows_of(c)].astype(F32) + add.total(c)
        stream[rows_of(c)] = total.astype(BF)
        spread.start(c)
    own = pltpu.make_async_copy(stream, columns, own_sem)
    own.start()
    fan.relay(5)
    for c in range(CH):
        spread.spread_pair(c)
    fan.relay(6)
    for c in range(CH):
        spread.relay(0, c)
    fan.last()
    for c in range(CH):
        spread.relay(1, c)
    fan.end()
    own.wait()
    for copy in kept:
        copy.wait()
    add.finish()
    spread.finish()
    fan.finish()


def reduce_only(part, base, encoded, *scratch):
    net = Narrow()
    greet(net.devices)
    add = Sum(net, part, scratch[:6], scratch[6:])
    add.start()
    for c in range(CH):
        add.forward(c)
    for c in range(CH):
        add.cross(c)
    for c in range(CH):
        total = base[rows_of(c)].astype(F32) + add.total(c)
        encoded[rows_of(c)] = total.astype(BF)
    add.finish()


def call_reduce_and_gather(part, cell, shares):
    rows, width = cell.shape
    panel = jax.ShapeDtypeStruct((NZ, 2, 1, 64, 512), BF)
    stream, gath, *outs = pl.pallas_call(
        reduce_and_gather,
        name="reduce_and_gather",
        out_shape=[
            jax.ShapeDtypeStruct((rows, width), BF),
            jax.ShapeDtypeStruct((rows, width * NN), BF),
            panel,
            panel,
        ],
        in_specs=[VM] * 3,
        out_specs=[VM] * 4,
        scratch_shapes=[DMA, DMA((2,))] + SUM_SCRATCH + GATHER_SCRATCH + fan_scratch(2),
        compiler_params=pltpu.CompilerParams(
            collective_id=1, has_side_effects=True, vmem_limit_bytes=LIMIT
        ),
    )(part, cell, shares)
    return [stream, gath] + [o.reshape(2048, 512) for o in outs]


def call_reduce_only(part, base):
    rows, width = base.shape
    return pl.pallas_call(
        reduce_only,
        name="reduce_only",
        out_shape=jax.ShapeDtypeStruct((rows, width), BF),
        in_specs=[VM] * 2,
        out_specs=VM,
        scratch_shapes=SUM_SCRATCH,
        compiler_params=pltpu.CompilerParams(
            collective_id=2, has_side_effects=True, vmem_limit_bytes=LIMIT
        ),
    )(part, base)


def extended(shard, axis, width):
    size, length = (lax.axis_size(axis), shard.shape[0])
    up = [(i, (i + 1) % size) for i in range(size - 1)]
    down = [(j, i) for i, j in up]
    before = lax.ppermute(shard[length - width :], axis, up)
    after = lax.ppermute(shard[:width], axis, down)
    return jnp.concatenate([before, shard, after], axis=0)


def rms_scale(values, gain):
    mean_square = jnp.mean(values * values, axis=-1, keepdims=True)
    return values * lax.rsqrt(mean_square + epsilon) * gain


def block_mask(layout, query_index):
    wanted = query_index[:, None] + jnp.arange(5, dtype=jnp.int32)[None, :] - 2
    return jnp.any(layout[:, :, None] == wanted[:, None, :], axis=1)


def on_device(cell_rows, attn_gain, ffn_gain, panels, panel_slot, layout):
    row_count = cell_rows.shape[0]
    block_count = row_count // BLK
    cell_full, attn_panel, shares = gather_all(cell_rows, panels[0], panel_slot)
    normed = rms_scale(cell_full.astype(F32), attn_gain).astype(BF)
    projected = jnp.dot(
        normed, attn_panel[:, : 3 * HD], preferred_element_type=F32
    ).astype(BF)
    key_window = extended(projected[:, HD:], "wide", 2 * BLK)
    pair_blocks = key_window.reshape(block_count + 4, BLK, 2, HD)
    stacked = jnp.stack([pair_blocks[o : o + block_count] for o in range(5)], axis=1)
    query_index = (
        lax.axis_index("wide") * block_count
        + jnp.arange(block_count, dtype=jnp.int32)
        + block_count // 2
    ) % NET_BLOCKS
    allowed = block_mask(layout, query_index)
    queries = projected[:, :HD].reshape(block_count, BLK, HD)
    scores = jnp.einsum(
        "bqc,bokc->bqok", queries, stacked[:, :, :, 0, :], preferred_element_type=F32
    ) * HD ** (-0.5)
    lifted = jnp.where(allowed[:, None, :, None], jnp.exp(scores), F32(0.0))
    weights = (lifted / jnp.sum(lifted, axis=(2, 3), keepdims=True)).astype(BF)
    head_out = jnp.einsum(
        "bqok,bokc->bqc", weights, stacked[:, :, :, 1, :], preferred_element_type=F32
    ).astype(BF)
    partial_value = lax.dot_general(
        head_out.reshape(row_count, HD), attn_panel[:, 3 * HD :],
        (((1,), (1,)), ((), ())), preferred_element_type=F32,
    ).astype(BF)
    stream, stream_full, up_panel, down_panel = call_reduce_and_gather(
        partial_value, cell_rows, shares
    )
    normed_ffn = rms_scale(stream_full.astype(F32), ffn_gain).astype(BF)
    hidden = jax.nn.gelu(
        jnp.dot(normed_ffn, up_panel, preferred_element_type=F32), approximate=False
    ).astype(BF)
    ffn_part = lax.dot_general(
        hidden, down_panel, (((1,), (1,)), ((), ())), preferred_element_type=F32
    ).astype(BF)
    return call_reduce_only(ffn_part, stream)


def solution(mesh):
    return jax.shard_map(
        on_device,
        mesh=mesh,
        in_specs=(P("wide", "narrow"), P(), P(), P("wide", None, "narrow"), P(), P("wide", None)),
        out_specs=P("wide", "narrow"),
        check_vma=False,
    )
```

```python
import functools

import jax
import jax.numpy as jnp
from jax import lax
from jax.experimental import pallas as pl
from jax.experimental.pallas import tpu as pltpu
from jax.sharding import PartitionSpec as P

HD = 128
BLK = 128
NET_BLOCKS = 32
NZ = 16
NW = 64
NN = 8
UP = 8
DOWN = 7
epsilon = 1e-05

BF = jnp.bfloat16
F32 = jnp.float32
VM = pl.BlockSpec(memory_space=pltpu.VMEM)
SM = pl.BlockSpec(memory_space=pltpu.SMEM)
DMA = pltpu.SemaphoreType.DMA
LIMIT = 60 * 1024 * 1024


def remote(src, dst, send, recv, wide, narrow):
    return pltpu.make_async_remote_copy(
        src_ref=src, dst_ref=dst, send_sem=send, recv_sem=recv,
        device_id=(wide, narrow), device_id_type=pl.DeviceIdType.MESH,
    )


def greet(devices):
    barrier = pltpu.get_barrier_semaphore()
    for wide, narrow in devices:
        pl.semaphore_signal(
            barrier, inc=1, device_id=(wide, narrow), device_id_type=pl.DeviceIdType.MESH
        )
    pl.semaphore_wait(barrier, len(devices))


def loop(low, high, body):
    def step(s, carry):
        body(s)
        return carry

    lax.fori_loop(low, high, step, 0)


class Place:
    def __init__(self):
        self.w, self.n = lax.axis_index("wide"), lax.axis_index("narrow")
        self.core, self.chip = self.w % 2, self.w // 2
        self.z, self.yl = self.chip % NZ, self.w // (2 * NZ)
        self.above = (self.at_z(self.z + 1), self.n)
        self.below = (self.at_z(self.z - 1), self.n)
        self.partner = (self.w + 1 - 2 * self.core, self.n)
        self.across = ((self.w + 2 * NZ) % NW, self.n)

    def at_z(self, zz):
        return (self.yl * NZ + (zz + NZ) % NZ) * 2 + self.core


class Pick:
    def __init__(self, at, panel, slots, bufs, sems):
        self.at, self.panel, self.slots = at, panel, slots
        self.cbuf, self.rsp, self.rsm, self.ysend, self.yrecv = bufs
        self.csem, self.psend, self.precv, self.msend, self.mrecv, self.ysem = sems
        self.parts = panel.shape[2]
        self.count = len(slots) * self.parts

    def owner(self, i):
        return self.slots[i // self.parts]

    def chip_data(self, i, j):
        part = i % self.parts
        return jnp.where(
            self.owner(i) % 2 == self.at.core,
            self.panel[j, self.at.core, part],
            self.cbuf[j, part],
        )

    def here(self, i, mine, other):
        return jnp.where(self.owner(i) // 2 == self.at.chip, mine, other)

    def up(self, s, i):
        return remote(
            self.rsp.at[s, i], self.rsp.at[s + 1, i],
            self.psend.at[s, i], self.precv.at[s, i], *self.at.above,
        )

    def down(self, s, i):
        return remote(
            self.rsm.at[s, i], self.rsm.at[s + 1, i],
            self.msend.at[s, i], self.mrecv.at[s, i], *self.at.below,
        )

    def swap(self, i):
        return remote(
            self.ysend.at[i], self.yrecv.at[i],
            self.ysem.at[0, i], self.ysem.at[1, i], *self.at.across,
        )

    def to_partner(self):
        return remote(
            self.panel.at[:, 1 - self.at.core], self.cbuf,
            self.csem.at[0], self.csem.at[1], *self.at.partner,
        )

    def begin(self, i):
        self.rsp[0, i] = self.chip_data(i, (self.at.z + UP) % NZ)
        self.up(0, i).start()
        self.rsm[0, i] = self.chip_data(i, (self.at.z + NZ - DOWN) % NZ)
        self.down(0, i).start()

    def merge_up(self, s, i):
        self.up(s - 1, i).wait_recv()
        mine = self.chip_data(i, (self.at.z + UP - s) % NZ)
        self.rsp[s, i] = self.here(i, mine, self.rsp[s, i])
        self.up(s, i).start()

    def merge_down(self, s, i):
        self.down(s - 1, i).wait_recv()
        mine = self.chip_data(i, (self.at.z + NZ - DOWN + s) % NZ)
        self.rsm[s, i] = self.here(i, mine, self.rsm[s, i])
        self.down(s, i).start()

    def end(self, i):
        self.up(UP - 1, i).wait_recv()
        self.down(DOWN - 1, i).wait_recv()
        behind = (self.at.z - (self.owner(i) // 2) % NZ + NZ) % NZ
        ring = jnp.where(behind <= UP, self.rsp[UP, i], self.rsm[DOWN, i])
        self.ysend[i] = self.here(i, self.chip_data(i, self.at.z), ring)
        self.swap(i).start()

    def result(self, i):
        self.swap(i).wait_recv()
        return jnp.where(
            self.owner(i) // (2 * NZ) == self.at.yl, self.ysend[i], self.yrecv[i]
        )

    def finish(self):
        self.to_partner().wait_send()

        def sent(s):
            for i in range(self.count):
                self.up(s, i).wait_send()

        def sent_down(s):
            for i in range(self.count):
                self.down(s, i).wait_send()

        loop(0, UP, sent)
        loop(0, DOWN, sent_down)
        for i in range(self.count):
            self.swap(i).wait_send()


class Fan:
    def __init__(self, at, outs, sems):
        self.at, self.outs = at, outs
        self.gpsend, self.gprecv, self.gmsend, self.gmrecv, self.xsend, self.xrecv = sems
        self.parts = outs[0].shape[2]
        self.streams = range(len(outs) * self.parts)

    def place(self, chunk, i):
        return self.outs[i // self.parts].at[(chunk + NZ) % NZ, self.at.core, i % self.parts]

    def up(self, s, i, source=None):
        part = self.place(self.at.z - s, i)
        source = part if source is None else source
        return remote(source, part, self.gpsend.at[s, i], self.gprecv.at[s, i], *self.at.above)

    def down(self, s, i, source=None):
        part = self.place(self.at.z + s, i)
        source = part if source is None else source
        return remote(source, part, self.gmsend.at[s, i], self.gmrecv.at[s, i], *self.at.below)

    def hand(self, order, chunk, i, source=None):
        part = self.place(chunk, i)
        source = part if source is None else source
        return remote(
            source, part, self.xsend.at[order, i], self.xrecv.at[order, i], *self.at.partner
        )

    def begin(self, i, source=None):
        self.up(0, i, source).start()
        self.down(0, i, source).start()
        self.hand(0, self.at.z, i, source).start()

    def relay_up(self, s, i):
        self.up(s - 1, i).wait_recv()
        self.up(s, i).start()
        self.hand(s, self.at.z - s, i).start()

    def relay_down(self, s, i):
        self.down(s - 1, i).wait_recv()
        self.down(s, i).start()
        self.hand(UP + s, self.at.z + s, i).start()

    def relay(self, s):
        for i in self.streams:
            self.relay_up(s, i)
            self.relay_down(s, i)

    def last(self):
        for i in self.streams:
            self.relay_up(DOWN, i)

    def end(self):
        for i in self.streams:
            self.up(UP - 1, i).wait_recv()
            self.hand(UP, self.at.z - UP, i).start()
            self.down(DOWN - 1, i).wait_recv()
            self.hand(UP + DOWN, self.at.z + DOWN, i).start()

    def finish(self):
        def sent(s):
            for i in self.streams:
                self.up(s, i).wait_send()

        def sent_down(s):
            for i in self.streams:
                self.down(s, i).wait_send()

        def handed(order):
            for i in self.streams:
                self.hand(order, self.at.z, i).wait()

        loop(0, UP, sent)
        loop(0, DOWN, sent_down)
        loop(0, NZ, handed)


PARTS = 2


def pick_scratch():
    piece = (64 // PARTS, 512)
    count = 3 * PARTS
    ups, downs = DMA((UP, count)), DMA((DOWN, count))
    return [
        pltpu.VMEM((NZ, PARTS) + piece, BF),
        pltpu.VMEM((UP + 1, count) + piece, BF),
        pltpu.VMEM((DOWN + 1, count) + piece, BF),
        pltpu.VMEM((count,) + piece, BF),
        pltpu.VMEM((count,) + piece, BF),
        DMA((2,)), ups, ups, downs, downs, DMA((2, count)),
    ]


def fan_scratch(count):
    ups, downs, hands = DMA((UP, count)), DMA((DOWN, count)), DMA((NZ, count))
    return [ups, ups, downs, downs, hands, hands]


def panels_and_cells(cell, panel, slot, gath, out, shares, *scratch):
    at = Place()
    pick = Pick(at, panel, [slot[i] for i in range(3)], scratch[:5], scratch[5:11])
    fan = Fan(at, [out], scratch[11:17])
    own_sem, nsend, nrecv = scratch[17:]
    w, n = at.w, at.n
    peers = [(n + k) % NN for k in range(1, NN)]
    greet([at.partner, at.above, at.below, at.across] + [(w, p) for p in peers])
    pick.to_partner().start()
    columns = gath.at[:, pl.ds(pl.multiple_of(n * 256, 256), 256)]
    own = pltpu.make_async_copy(cell, columns, own_sem)
    own.start()
    first = range(2 * PARTS)
    later = range(2 * PARTS, 3 * PARTS)
    pick.to_partner().wait_recv()
    for i in first:
        pick.begin(i)
    sends = []
    for k in range(1, NN):
        copy = remote(cell, columns, nsend.at[k - 1], nrecv.at[k - 1], w, peers[k - 1])
        copy.start()
        sends.append(copy)

    def both(s):
        for i in first:
            pick.merge_up(s, i)
            pick.merge_down(s, i)

    loop(1, DOWN, both)
    for i in first:
        pick.merge_up(UP - 1, i)
    for i in first:
        pick.end(i)
    for i in range(PARTS):
        out[at.z, at.core, i] = pick.result(i)
        fan.begin(i)
    for i in later:
        pick.begin(i)

    def mixed(s):
        fan.relay(s)
        for i in later:
            pick.merge_up(s, i)
            pick.merge_down(s, i)

    loop(1, DOWN, mixed)
    fan.last()
    for i in later:
        pick.merge_up(UP - 1, i)
    fan.end()
    for i in later:
        pick.end(i)
    for i in range(PARTS, 3 * PARTS):
        shares[i - PARTS] = pick.result(i)
    own.wait()
    for copy in sends:
        copy.wait()
    pick.finish()
    fan.finish()


def gather_all(cell_rows, panel, panel_slot):
    rows, width = cell_rows.shape
    shape = (NZ, 2, PARTS, 64 // PARTS, 512)
    gath, out, shares = pl.pallas_call(
        panels_and_cells,
        name="panels_and_cells",
        out_shape=[
            jax.ShapeDtypeStruct((rows, width * NN), BF),
            jax.ShapeDtypeStruct(shape, BF),
            jax.ShapeDtypeStruct((2 * PARTS, 64 // PARTS, 512), BF),
        ],
        in_specs=[VM, VM, SM],
        out_specs=[VM] * 3,
        scratch_shapes=pick_scratch()
        + fan_scratch(PARTS)
        + [DMA, DMA((NN - 1,)), DMA((NN - 1,))],
        compiler_params=pltpu.CompilerParams(
            collective_id=0, has_side_effects=True, vmem_limit_bytes=LIMIT
        ),
    )(cell_rows, panel.reshape(shape), panel_slot)
    return gath, out.reshape(2048, 512), shares.reshape(2, 64, 512)


class Narrow:
    def __init__(self):
        self.w, self.n = lax.axis_index("wide"), lax.axis_index("narrow")
        self.x, self.h = self.n // 2, self.n % 2
        self.right = (self.w, (self.n + 2) % NN)
        self.left = (self.w, (self.n + NN - 2) % NN)
        self.pair = (self.w, self.n + 1 - 2 * self.h)
        self.devices = [self.right, self.left, self.pair]


CH = 8
HALF = CH // 2
ROWS = 512 // CH


def rows_of(c):
    return pl.ds(c * ROWS, ROWS)


class Sum:
    def __init__(self, net, part, bufs, sems):
        self.net, self.part = net, part
        self.far, self.relay, self.near_r, self.near_l, self.ysend, self.yrecv = bufs
        self.fs, self.fr, self.rs, self.rr, self.ls, self.lr, self.ys, self.yr = sems

    def block(self, x, c):
        start = pl.multiple_of(((x + 4) % 4) * 512, 512)
        return self.part.at[rows_of(c), pl.ds(start, 512)]

    def to_far(self, c):
        target = self.net.right if c % 2 == 0 else self.net.left
        return remote(
            self.block(self.net.x + 2, c), self.far.at[c], self.fs.at[c], self.fr.at[c], *target
        )

    def to_right(self, c):
        source = self.relay.at[c] if c % 2 == 0 else self.block(self.net.x + 1, c)
        return remote(source, self.near_r.at[c], self.rs.at[c], self.rr.at[c], *self.net.right)

    def to_left(self, c):
        source = self.relay.at[c] if c % 2 == 1 else self.block(self.net.x - 1, c)
        return remote(source, self.near_l.at[c], self.ls.at[c], self.lr.at[c], *self.net.left)

    def to_pair(self, c):
        return remote(
            self.ysend.at[c], self.yrecv.at[c], self.ys.at[c], self.yr.at[c], *self.net.pair
        )

    def start(self):
        for c in range(CH):
            self.to_far(c).start()

    def forward(self, c):
        self.to_far(c).wait_recv()
        step = 1 if c % 2 == 0 else -1
        mine = self.block(self.net.x + step, c)[...]
        self.relay[c] = (mine.astype(F32) + self.far[c].astype(F32)).astype(BF)
        self.to_right(c).start()
        self.to_left(c).start()

    def columns(self, c, h):
        start = pl.multiple_of((self.net.x * 2 + h) * 256, 256)
        cols = pl.ds(pl.multiple_of(h * 256, 256), 256)
        total = self.part[rows_of(c), pl.ds(start, 256)].astype(F32)
        total = total + self.near_r[c, :, cols].astype(F32)
        return total + self.near_l[c, :, cols].astype(F32)

    def cross(self, c):
        self.to_right(c).wait_recv()
        self.to_left(c).wait_recv()
        self.ysend[c] = self.columns(c, 1 - self.net.h).astype(BF)
        self.to_pair(c).start()

    def total(self, c):
        self.to_pair(c).wait_recv()
        return self.columns(c, self.net.h) + self.yrecv[c].astype(F32)

    def finish(self):
        for c in range(CH):
            self.to_far(c).wait_send()
            self.to_right(c).wait_send()
            self.to_left(c).wait_send()
            self.to_pair(c).wait_send()


SUM_SCRATCH = (
    [pltpu.VMEM((CH, ROWS, 512), BF)] * 4
    + [pltpu.VMEM((CH, ROWS, 256), BF)] * 2
    + [DMA((CH,))] * 8
)


class Gather:
    def __init__(self, net, piece, gath, sems):
        self.net, self.piece, self.gath = net, piece, gath
        self.ys, self.yr, self.rs, self.rr, self.ls, self.lr, self.fs, self.fr = sems

    def place(self, x, q, c):
        h = self.net.h if q == 0 else 1 - self.net.h
        start = pl.multiple_of((((x + 4) % 4) * 2 + h) * 256, 256)
        return self.gath.at[rows_of(c), pl.ds(start, 256)]

    def source(self, q, c):
        return self.piece.at[rows_of(c)] if q == 0 else self.place(self.net.x, 1, c)

    def to_pair(self, c):
        return remote(
            self.source(0, c), self.place(self.net.x, 0, c),
            self.ys.at[c], self.yr.at[c], *self.net.pair,
        )

    def to_right(self, q, c):
        return remote(
            self.source(q, c), self.place(self.net.x, q, c),
            self.rs.at[q, c], self.rr.at[q, c], *self.net.right,
        )

    def to_left(self, q, c):
        return remote(
            self.source(q, c), self.place(self.net.x, q, c),
            self.ls.at[q, c], self.lr.at[q, c], *self.net.left,
        )

    def onward(self, q, c):
        step, target = (-1, self.net.right) if c % 2 == 0 else (1, self.net.left)
        part = self.place(self.net.x + step, q, c)
        return remote(part, part, self.fs.at[q, c], self.fr.at[q, c], *target)

    def start(self, c):
        self.to_pair(c).start()
        self.to_right(0, c).start()
        self.to_left(0, c).start()

    def spread_pair(self, c):
        self.to_pair(c).wait_recv()
        self.to_right(1, c).start()
        self.to_left(1, c).start()

    def relay(self, q, c):
        self.to_right(q, c).wait_recv()
        self.to_left(q, c).wait_recv()
        self.onward(q, c).start()

    def finish(self):
        for c in range(CH):
            self.to_pair(c).wait_send()
            for q in range(2):
                self.to_right(q, c).wait_send()
                self.to_left(q, c).wait_send()
                self.onward(q, c).wait()


GATHER_SCRATCH = [DMA((CH,))] * 2 + [DMA((2, CH))] * 6


def reduce_and_gather(part, cell, shares, stream, gath, out0, out1, own_sem, share_sem, *scratch):
    net = Narrow()
    at = Place()
    greet(net.devices + [at.partner, at.above, at.below])
    add = Sum(net, part, scratch[:6], scratch[6:14])
    spread = Gather(net, stream, gath, scratch[14:22])
    fan = Fan(at, [out0, out1], scratch[22:])
    add.start()
    kept = []
    for i in fan.streams:
        fan.begin(i, shares.at[i])
        copy = pltpu.make_async_copy(shares.at[i], fan.place(at.z, i), share_sem.at[i])
        copy.start()
        kept.append(copy)
    for c in range(CH):
        add.forward(c)
        if c % HALF == HALF - 1:
            fan.relay(c // HALF + 1)
    for c in range(CH):
        add.cross(c)
        if c % HALF == HALF - 1:
            fan.relay(c // HALF + 3)
    columns = gath.at[:, pl.ds(pl.multiple_of(net.n * 256, 256), 256)]
    for c in range(CH):
        total = cell[rows_of(c)].astype(F32) + add.total(c)
        stream[rows_of(c)] = total.astype(BF)
        spread.start(c)
    own = pltpu.make_async_copy(stream, columns, own_sem)
    own.start()
    fan.relay(5)
    for c in range(CH):
        spread.spread_pair(c)
    fan.relay(6)
    for c in range(CH):
        spread.relay(0, c)
    fan.last()
    for c in range(CH):
        spread.relay(1, c)
    fan.end()
    own.wait()
    for copy in kept:
        copy.wait()
    add.finish()
    spread.finish()
    fan.finish()


def reduce_only(part, base, encoded, *scratch):
    net = Narrow()
    greet(net.devices)
    add = Sum(net, part, scratch[:6], scratch[6:])
    add.start()
    for c in range(CH):
        add.forward(c)
    for c in range(CH):
        add.cross(c)
    for c in range(CH):
        total = base[rows_of(c)].astype(F32) + add.total(c)
        encoded[rows_of(c)] = total.astype(BF)
    add.finish()


def call_reduce_and_gather(part, cell, shares):
    rows, width = cell.shape
    panel = jax.ShapeDtypeStruct((NZ, 2, 1, 64, 512), BF)
    stream, gath, *outs = pl.pallas_call(
        reduce_and_gather,
        name="reduce_and_gather",
        out_shape=[
            jax.ShapeDtypeStruct((rows, width), BF),
            jax.ShapeDtypeStruct((rows, width * NN), BF),
            panel,
            panel,
        ],
        in_specs=[VM] * 3,
        out_specs=[VM] * 4,
        scratch_shapes=[DMA, DMA((2,))] + SUM_SCRATCH + GATHER_SCRATCH + fan_scratch(2),
        compiler_params=pltpu.CompilerParams(
            collective_id=1, has_side_effects=True, vmem_limit_bytes=LIMIT
        ),
    )(part, cell, shares)
    return [stream, gath] + [o.reshape(2048, 512) for o in outs]


def call_reduce_only(part, base):
    rows, width = base.shape
    return pl.pallas_call(
        reduce_only,
        name="reduce_only",
        out_shape=jax.ShapeDtypeStruct((rows, width), BF),
        in_specs=[VM] * 2,
        out_specs=VM,
        scratch_shapes=SUM_SCRATCH,
        compiler_params=pltpu.CompilerParams(
            collective_id=2, has_side_effects=True, vmem_limit_bytes=LIMIT
        ),
    )(part, base)


def extended(shard, axis, width):
    size, length = (lax.axis_size(axis), shard.shape[0])
    up = [(i, (i + 1) % size) for i in range(size - 1)]
    down = [(j, i) for i, j in up]
    before = lax.ppermute(shard[length - width :], axis, up)
    after = lax.ppermute(shard[:width], axis, down)
    return jnp.concatenate([before, shard, after], axis=0)


def rms_scale(values, gain):
    mean_square = jnp.mean(values * values, axis=-1, keepdims=True)
    return values * lax.rsqrt(mean_square + epsilon) * gain


def block_mask(layout, query_index):
    wanted = query_index[:, None] + jnp.arange(5, dtype=jnp.int32)[None, :] - 2
    return jnp.any(layout[:, :, None] == wanted[:, None, :], axis=1)


def on_device(cell_rows, attn_gain, ffn_gain, panels, panel_slot, layout):
    row_count = cell_rows.shape[0]
    block_count = row_count // BLK
    cell_full, attn_panel, shares = gather_all(cell_rows, panels[0], panel_slot)
    normed = rms_scale(cell_full.astype(F32), attn_gain).astype(BF)
    projected = jnp.dot(
        normed, attn_panel[:, : 3 * HD], preferred_element_type=F32
    ).astype(BF)
    key_window = extended(projected[:, HD:], "wide", 2 * BLK)
    pair_blocks = key_window.reshape(block_count + 4, BLK, 2, HD)
    stacked = jnp.stack([pair_blocks[o : o + block_count] for o in range(5)], axis=1)
    query_index = (
        lax.axis_index("wide") * block_count
        + jnp.arange(block_count, dtype=jnp.int32)
        + block_count // 2
    ) % NET_BLOCKS
    allowed = block_mask(layout, query_index)
    queries = projected[:, :HD].reshape(block_count, BLK, HD)
    scores = jnp.einsum(
        "bqc,bokc->bqok", queries, stacked[:, :, :, 0, :], preferred_element_type=F32
    ) * HD ** (-0.5)
    lifted = jnp.where(allowed[:, None, :, None], jnp.exp(scores), F32(0.0))
    weights = (lifted / jnp.sum(lifted, axis=(2, 3), keepdims=True)).astype(BF)
    head_out = jnp.einsum(
        "bqok,bokc->bqc", weights, stacked[:, :, :, 1, :], preferred_element_type=F32
    ).astype(BF)
    partial_value = lax.dot_general(
        head_out.reshape(row_count, HD), attn_panel[:, 3 * HD :],
        (((1,), (1,)), ((), ())), preferred_element_type=F32,
    ).astype(BF)
    stream, stream_full, up_panel, down_panel = call_reduce_and_gather(
        partial_value, cell_rows, shares
    )
    normed_ffn = rms_scale(stream_full.astype(F32), ffn_gain).astype(BF)
    hidden = jax.nn.gelu(
        jnp.dot(normed_ffn, up_panel, preferred_element_type=F32), approximate=False
    ).astype(BF)
    ffn_part = lax.dot_general(
        hidden, down_panel, (((1,), (1,)), ((), ())), preferred_element_type=F32
    ).astype(BF)
    return call_reduce_only(ffn_part, stream)


def solution(mesh):
    return jax.shard_map(
        on_device,
        mesh=mesh,
        in_specs=(P("wide", "narrow"), P(), P(), P("wide", None, "narrow"), P(), P("wide", None)),
        out_specs=P("wide", "narrow"),
        check_vma=False,
    )
```

```python
import functools

import jax
import jax.numpy as jnp
from jax import lax
from jax.experimental import pallas as pl
from jax.experimental.pallas import tpu as pltpu
from jax.sharding import PartitionSpec as P

HD = 128
BLK = 128
NET_BLOCKS = 32
NZ = 16
NW = 64
NN = 8
UP = 8
DOWN = 7
epsilon = 1e-05

BF = jnp.bfloat16
F32 = jnp.float32
VM = pl.BlockSpec(memory_space=pltpu.VMEM)
SM = pl.BlockSpec(memory_space=pltpu.SMEM)
DMA = pltpu.SemaphoreType.DMA
LIMIT = 60 * 1024 * 1024


def remote(src, dst, send, recv, wide, narrow):
    return pltpu.make_async_remote_copy(
        src_ref=src, dst_ref=dst, send_sem=send, recv_sem=recv,
        device_id=(wide, narrow), device_id_type=pl.DeviceIdType.MESH,
    )


def greet(devices):
    barrier = pltpu.get_barrier_semaphore()
    for wide, narrow in devices:
        pl.semaphore_signal(
            barrier, inc=1, device_id=(wide, narrow), device_id_type=pl.DeviceIdType.MESH
        )
    pl.semaphore_wait(barrier, len(devices))


def loop(low, high, body):
    def step(s, carry):
        body(s)
        return carry

    lax.fori_loop(low, high, step, 0)


class Place:
    def __init__(self):
        self.w, self.n = lax.axis_index("wide"), lax.axis_index("narrow")
        self.core, self.chip = self.w % 2, self.w // 2
        self.z, self.yl = self.chip % NZ, self.w // (2 * NZ)
        self.above = (self.at_z(self.z + 1), self.n)
        self.below = (self.at_z(self.z - 1), self.n)
        self.partner = (self.w + 1 - 2 * self.core, self.n)
        self.across = ((self.w + 2 * NZ) % NW, self.n)

    def at_z(self, zz):
        return (self.yl * NZ + (zz + NZ) % NZ) * 2 + self.core


class Pick:
    def __init__(self, at, panel, slots, bufs, sems):
        self.at, self.panel, self.slots = at, panel, slots
        self.cbuf, self.rsp, self.rsm, self.ysend, self.yrecv = bufs
        self.csem, self.psend, self.precv, self.msend, self.mrecv, self.ysem = sems
        self.parts = panel.shape[2]
        self.count = len(slots) * self.parts

    def owner(self, i):
        return self.slots[i // self.parts]

    def chip_data(self, i, j):
        part = i % self.parts
        return jnp.where(
            self.owner(i) % 2 == self.at.core,
            self.panel[j, self.at.core, part],
            self.cbuf[j, part],
        )

    def here(self, i, mine, other):
        return jnp.where(self.owner(i) // 2 == self.at.chip, mine, other)

    def up(self, s, i):
        return remote(
            self.rsp.at[s, i], self.rsp.at[s + 1, i],
            self.psend.at[s, i], self.precv.at[s, i], *self.at.above,
        )

    def down(self, s, i):
        return remote(
            self.rsm.at[s, i], self.rsm.at[s + 1, i],
            self.msend.at[s, i], self.mrecv.at[s, i], *self.at.below,
        )

    def swap(self, i):
        return remote(
            self.ysend.at[i], self.yrecv.at[i],
            self.ysem.at[0, i], self.ysem.at[1, i], *self.at.across,
        )

    def to_partner(self):
        return remote(
            self.panel.at[:, 1 - self.at.core], self.cbuf,
            self.csem.at[0], self.csem.at[1], *self.at.partner,
        )

    def begin(self, i):
        self.rsp[0, i] = self.chip_data(i, (self.at.z + UP) % NZ)
        self.up(0, i).start()
        self.rsm[0, i] = self.chip_data(i, (self.at.z + NZ - DOWN) % NZ)
        self.down(0, i).start()

    def merge_up(self, s, i):
        self.up(s - 1, i).wait_recv()
        mine = self.chip_data(i, (self.at.z + UP - s) % NZ)
        self.rsp[s, i] = self.here(i, mine, self.rsp[s, i])
        self.up(s, i).start()

    def merge_down(self, s, i):
        self.down(s - 1, i).wait_recv()
        mine = self.chip_data(i, (self.at.z + NZ - DOWN + s) % NZ)
        self.rsm[s, i] = self.here(i, mine, self.rsm[s, i])
        self.down(s, i).start()

    def end(self, i):
        self.up(UP - 1, i).wait_recv()
        self.down(DOWN - 1, i).wait_recv()
        behind = (self.at.z - (self.owner(i) // 2) % NZ + NZ) % NZ
        ring = jnp.where(behind <= UP, self.rsp[UP, i], self.rsm[DOWN, i])
        self.ysend[i] = self.here(i, self.chip_data(i, self.at.z), ring)
        self.swap(i).start()

    def result(self, i):
        self.swap(i).wait_recv()
        return jnp.where(
            self.owner(i) // (2 * NZ) == self.at.yl, self.ysend[i], self.yrecv[i]
        )

    def finish(self):
        self.to_partner().wait_send()

        def sent(s):
            for i in range(self.count):
                self.up(s, i).wait_send()

        def sent_down(s):
            for i in range(self.count):
                self.down(s, i).wait_send()

        loop(0, UP, sent)
        loop(0, DOWN, sent_down)
        for i in range(self.count):
            self.swap(i).wait_send()


class Fan:
    def __init__(self, at, outs, sems):
        self.at, self.outs = at, outs
        self.gpsend, self.gprecv, self.gmsend, self.gmrecv, self.xsend, self.xrecv = sems
        self.parts = outs[0].shape[2]
        self.streams = range(len(outs) * self.parts)

    def place(self, chunk, i):
        return self.outs[i // self.parts].at[(chunk + NZ) % NZ, self.at.core, i % self.parts]

    def up(self, s, i, source=None):
        part = self.place(self.at.z - s, i)
        source = part if source is None else source
        return remote(source, part, self.gpsend.at[s, i], self.gprecv.at[s, i], *self.at.above)

    def down(self, s, i, source=None):
        part = self.place(self.at.z + s, i)
        source = part if source is None else source
        return remote(source, part, self.gmsend.at[s, i], self.gmrecv.at[s, i], *self.at.below)

    def hand(self, order, chunk, i, source=None):
        part = self.place(chunk, i)
        source = part if source is None else source
        return remote(
            source, part, self.xsend.at[order, i], self.xrecv.at[order, i], *self.at.partner
        )

    def begin(self, i, source=None):
        self.up(0, i, source).start()
        self.down(0, i, source).start()
        self.hand(0, self.at.z, i, source).start()

    def relay_up(self, s, i):
        self.up(s - 1, i).wait_recv()
        self.up(s, i).start()
        self.hand(s, self.at.z - s, i).start()

    def relay_down(self, s, i):
        self.down(s - 1, i).wait_recv()
        self.down(s, i).start()
        self.hand(UP + s, self.at.z + s, i).start()

    def relay(self, s):
        for i in self.streams:
            self.relay_up(s, i)
            self.relay_down(s, i)

    def last(self):
        for i in self.streams:
            self.relay_up(DOWN, i)

    def end(self):
        for i in self.streams:
            self.up(UP - 1, i).wait_recv()
            self.hand(UP, self.at.z - UP, i).start()
            self.down(DOWN - 1, i).wait_recv()
            self.hand(UP + DOWN, self.at.z + DOWN, i).start()

    def finish(self):
        def sent(s):
            for i in self.streams:
                self.up(s, i).wait_send()

        def sent_down(s):
            for i in self.streams:
                self.down(s, i).wait_send()

        def handed(order):
            for i in self.streams:
                self.hand(order, self.at.z, i).wait()

        loop(0, UP, sent)
        loop(0, DOWN, sent_down)
        loop(0, NZ, handed)


PARTS = 2


def pick_scratch():
    piece = (64 // PARTS, 512)
    count = 3 * PARTS
    ups, downs = DMA((UP, count)), DMA((DOWN, count))
    return [
        pltpu.VMEM((NZ, PARTS) + piece, BF),
        pltpu.VMEM((UP + 1, count) + piece, BF),
        pltpu.VMEM((DOWN + 1, count) + piece, BF),
        pltpu.VMEM((count,) + piece, BF),
        pltpu.VMEM((count,) + piece, BF),
        DMA((2,)), ups, ups, downs, downs, DMA((2, count)),
    ]


def fan_scratch(count):
    ups, downs, hands = DMA((UP, count)), DMA((DOWN, count)), DMA((NZ, count))
    return [ups, ups, downs, downs, hands, hands]


def panels_and_cells(cell, panel, slot, gath, out, shares, *scratch):
    at = Place()
    pick = Pick(at, panel, [slot[i] for i in range(3)], scratch[:5], scratch[5:11])
    fan = Fan(at, [out], scratch[11:17])
    own_sem, nsend, nrecv = scratch[17:]
    w, n = at.w, at.n
    peers = [(n + k) % NN for k in range(1, NN)]
    greet([at.partner, at.above, at.below, at.across] + [(w, p) for p in peers])
    pick.to_partner().start()
    columns = gath.at[:, pl.ds(pl.multiple_of(n * 256, 256), 256)]
    own = pltpu.make_async_copy(cell, columns, own_sem)
    own.start()
    first = range(2 * PARTS)
    later = range(2 * PARTS, 3 * PARTS)
    pick.to_partner().wait_recv()
    for i in first:
        pick.begin(i)
    sends = []
    for k in range(1, NN):
        copy = remote(cell, columns, nsend.at[k - 1], nrecv.at[k - 1], w, peers[k - 1])
        copy.start()
        sends.append(copy)

    def both(s):
        for i in first:
            pick.merge_up(s, i)
            pick.merge_down(s, i)

    loop(1, DOWN, both)
    for i in first:
        pick.merge_up(UP - 1, i)
    for i in first:
        pick.end(i)
    for i in range(PARTS):
        out[at.z, at.core, i] = pick.result(i)
        fan.begin(i)
    for i in later:
        pick.begin(i)

    def mixed(s):
        fan.relay(s)
        for i in later:
            pick.merge_up(s, i)
            pick.merge_down(s, i)

    loop(1, DOWN, mixed)
    fan.last()
    for i in later:
        pick.merge_up(UP - 1, i)
    fan.end()
    for i in later:
        pick.end(i)
    for i in range(PARTS, 3 * PARTS):
        shares[i - PARTS] = pick.result(i)
    own.wait()
    for copy in sends:
        copy.wait()
    pick.finish()
    fan.finish()


def gather_all(cell_rows, panel, panel_slot):
    rows, width = cell_rows.shape
    shape = (NZ, 2, PARTS, 64 // PARTS, 512)
    gath, out, shares = pl.pallas_call(
        panels_and_cells,
        name="panels_and_cells",
        out_shape=[
            jax.ShapeDtypeStruct((rows, width * NN), BF),
            jax.ShapeDtypeStruct(shape, BF),
            jax.ShapeDtypeStruct((2 * PARTS, 64 // PARTS, 512), BF),
        ],
        in_specs=[VM, VM, SM],
        out_specs=[VM] * 3,
        scratch_shapes=pick_scratch()
        + fan_scratch(PARTS)
        + [DMA, DMA((NN - 1,)), DMA((NN - 1,))],
        compiler_params=pltpu.CompilerParams(
            collective_id=0, has_side_effects=True, vmem_limit_bytes=LIMIT
        ),
    )(cell_rows, panel.reshape(shape), panel_slot)
    return gath, out.reshape(2048, 512), shares.reshape(2, 64, 512)


class Narrow:
    def __init__(self):
        self.w, self.n = lax.axis_index("wide"), lax.axis_index("narrow")
        self.x, self.h = self.n // 2, self.n % 2
        self.right = (self.w, (self.n + 2) % NN)
        self.left = (self.w, (self.n + NN - 2) % NN)
        self.pair = (self.w, self.n + 1 - 2 * self.h)
        self.devices = [self.right, self.left, self.pair]


CH = 4
HALF = CH // 2
ROWS = 512 // CH


def rows_of(c):
    return pl.ds(c * ROWS, ROWS)


class Sum:
    def __init__(self, net, part, bufs, sems):
        self.net, self.part = net, part
        self.far, self.relay, self.near_r, self.near_l, self.ysend, self.yrecv = bufs
        self.fs, self.fr, self.rs, self.rr, self.ls, self.lr, self.ys, self.yr = sems

    def block(self, x, c):
        start = pl.multiple_of(((x + 4) % 4) * 512, 512)
        return self.part.at[rows_of(c), pl.ds(start, 512)]

    def to_far(self, c):
        target = self.net.right if c % 2 == 0 else self.net.left
        return remote(
            self.block(self.net.x + 2, c), self.far.at[c], self.fs.at[c], self.fr.at[c], *target
        )

    def to_right(self, c):
        source = self.relay.at[c] if c % 2 == 0 else self.block(self.net.x + 1, c)
        return remote(source, self.near_r.at[c], self.rs.at[c], self.rr.at[c], *self.net.right)

    def to_left(self, c):
        source = self.relay.at[c] if c % 2 == 1 else self.block(self.net.x - 1, c)
        return remote(source, self.near_l.at[c], self.ls.at[c], self.lr.at[c], *self.net.left)

    def to_pair(self, c):
        return remote(
            self.ysend.at[c], self.yrecv.at[c], self.ys.at[c], self.yr.at[c], *self.net.pair
        )

    def start(self):
        for c in range(CH):
            self.to_far(c).start()

    def forward(self, c):
        self.to_far(c).wait_recv()
        step = 1 if c % 2 == 0 else -1
        mine = self.block(self.net.x + step, c)[...]
        self.relay[c] = (mine.astype(F32) + self.far[c].astype(F32)).astype(BF)
        self.to_right(c).start()
        self.to_left(c).start()

    def columns(self, c, h):
        start = pl.multiple_of((self.net.x * 2 + h) * 256, 256)
        cols = pl.ds(pl.multiple_of(h * 256, 256), 256)
        total = self.part[rows_of(c), pl.ds(start, 256)].astype(F32)
        total = total + self.near_r[c, :, cols].astype(F32)
        return total + self.near_l[c, :, cols].astype(F32)

    def cross(self, c):
        self.to_right(c).wait_recv()
        self.to_left(c).wait_recv()
        self.ysend[c] = self.columns(c, 1 - self.net.h).astype(BF)
        self.to_pair(c).start()

    def total(self, c):
        self.to_pair(c).wait_recv()
        return self.columns(c, self.net.h) + self.yrecv[c].astype(F32)

    def finish(self):
        for c in range(CH):
            self.to_far(c).wait_send()
            self.to_right(c).wait_send()
            self.to_left(c).wait_send()
            self.to_pair(c).wait_send()


SUM_SCRATCH = (
    [pltpu.VMEM((CH, ROWS, 512), BF)] * 4
    + [pltpu.VMEM((CH, ROWS, 256), BF)] * 2
    + [DMA((CH,))] * 8
)


class Gather:
    def __init__(self, net, piece, gath, sems):
        self.net, self.piece, self.gath = net, piece, gath
        self.ys, self.yr, self.rs, self.rr, self.ls, self.lr, self.fs, self.fr = sems

    def place(self, x, q, c):
        h = self.net.h if q == 0 else 1 - self.net.h
        start = pl.multiple_of((((x + 4) % 4) * 2 + h) * 256, 256)
        return self.gath.at[rows_of(c), pl.ds(start, 256)]

    def source(self, q, c):
        return self.piece.at[rows_of(c)] if q == 0 else self.place(self.net.x, 1, c)

    def to_pair(self, c):
        return remote(
            self.source(0, c), self.place(self.net.x, 0, c),
            self.ys.at[c], self.yr.at[c], *self.net.pair,
        )

    def to_right(self, q, c):
        return remote(
            self.source(q, c), self.place(self.net.x, q, c),
            self.rs.at[q, c], self.rr.at[q, c], *self.net.right,
        )

    def to_left(self, q, c):
        return remote(
            self.source(q, c), self.place(self.net.x, q, c),
            self.ls.at[q, c], self.lr.at[q, c], *self.net.left,
        )

    def onward(self, q, c):
        step, target = (-1, self.net.right) if c % 2 == 0 else (1, self.net.left)
        part = self.place(self.net.x + step, q, c)
        return remote(part, part, self.fs.at[q, c], self.fr.at[q, c], *target)

    def start(self, c):
        self.to_pair(c).start()
        self.to_right(0, c).start()
        self.to_left(0, c).start()

    def spread_pair(self, c):
        self.to_pair(c).wait_recv()
        self.to_right(1, c).start()
        self.to_left(1, c).start()

    def relay(self, q, c):
        self.to_right(q, c).wait_recv()
        self.to_left(q, c).wait_recv()
        self.onward(q, c).start()

    def finish(self):
        for c in range(CH):
            self.to_pair(c).wait_send()
            for q in range(2):
                self.to_right(q, c).wait_send()
                self.to_left(q, c).wait_send()
                self.onward(q, c).wait()


GATHER_SCRATCH = [DMA((CH,))] * 2 + [DMA((2, CH))] * 6


def reduce_and_gather(part, cell, shares, stream, gath, out0, out1, own_sem, share_sem, *scratch):
    net = Narrow()
    at = Place()
    greet(net.devices + [at.partner, at.above, at.below])
    add = Sum(net, part, scratch[:6], scratch[6:14])
    spread = Gather(net, stream, gath, scratch[14:22])
    fan = Fan(at, [out0, out1], scratch[22:])
    add.start()
    kept = []
    for i in fan.streams:
        fan.begin(i, shares.at[i])
        copy = pltpu.make_async_copy(shares.at[i], fan.place(at.z, i), share_sem.at[i])
        copy.start()
        kept.append(copy)
    for c in range(CH):
        add.forward(c)
        if c % HALF == HALF - 1:
            fan.relay(c // HALF + 1)
    for c in range(CH):
        add.cross(c)
        if c % HALF == HALF - 1:
            fan.relay(c // HALF + 3)
    columns = gath.at[:, pl.ds(pl.multiple_of(net.n * 256, 256), 256)]
    for c in range(CH):
        total = cell[rows_of(c)].astype(F32) + add.total(c)
        stream[rows_of(c)] = total.astype(BF)
        spread.start(c)
    own = pltpu.make_async_copy(stream, columns, own_sem)
    own.start()
    fan.relay(5)
    for c in range(CH):
        spread.spread_pair(c)
    fan.relay(6)
    for c in range(CH):
        spread.relay(0, c)
    fan.last()
    for c in range(CH):
        spread.relay(1, c)
    fan.end()
    own.wait()
    for copy in kept:
        copy.wait()
    add.finish()
    spread.finish()
    fan.finish()


def reduce_only(part, base, encoded, *scratch):
    net = Narrow()
    greet(net.devices)
    add = Sum(net, part, scratch[:6], scratch[6:])
    add.start()
    for c in range(CH):
        add.forward(c)
    for c in range(CH):
        add.cross(c)
    for c in range(CH):
        total = base[rows_of(c)].astype(F32) + add.total(c)
        encoded[rows_of(c)] = total.astype(BF)
    add.finish()


def call_reduce_and_gather(part, cell, shares):
    rows, width = cell.shape
    panel = jax.ShapeDtypeStruct((NZ, 2, 1, 64, 512), BF)
    stream, gath, *outs = pl.pallas_call(
        reduce_and_gather,
        name="reduce_and_gather",
        out_shape=[
            jax.ShapeDtypeStruct((rows, width), BF),
            jax.ShapeDtypeStruct((rows, width * NN), BF),
            panel,
            panel,
        ],
        in_specs=[VM] * 3,
        out_specs=[VM] * 4,
        scratch_shapes=[DMA, DMA((2,))] + SUM_SCRATCH + GATHER_SCRATCH + fan_scratch(2),
        compiler_params=pltpu.CompilerParams(
            collective_id=1, has_side_effects=True, vmem_limit_bytes=LIMIT
        ),
    )(part, cell, shares)
    return [stream, gath] + [o.reshape(2048, 512) for o in outs]


def call_reduce_only(part, base):
    rows, width = base.shape
    return pl.pallas_call(
        reduce_only,
        name="reduce_only",
        out_shape=jax.ShapeDtypeStruct((rows, width), BF),
        in_specs=[VM] * 2,
        out_specs=VM,
        scratch_shapes=SUM_SCRATCH,
        compiler_params=pltpu.CompilerParams(
            collective_id=2, has_side_effects=True, vmem_limit_bytes=LIMIT
        ),
    )(part, base)


def extended(shard, axis, width):
    size, length = (lax.axis_size(axis), shard.shape[0])
    up = [(i, (i + 1) % size) for i in range(size - 1)]
    down = [(j, i) for i, j in up]
    before = lax.ppermute(shard[length - width :], axis, up)
    after = lax.ppermute(shard[:width], axis, down)
    return jnp.concatenate([before, shard, after], axis=0)


def rms_scale(values, gain):
    mean_square = jnp.mean(values * values, axis=-1, keepdims=True)
    return values * lax.rsqrt(mean_square + epsilon) * gain


def block_mask(layout, query_index):
    wanted = query_index[:, None] + jnp.arange(5, dtype=jnp.int32)[None, :] - 2
    return jnp.any(layout[:, :, None] == wanted[:, None, :], axis=1)


def on_device(cell_rows, attn_gain, ffn_gain, panels, panel_slot, layout):
    row_count = cell_rows.shape[0]
    block_count = row_count // BLK
    cell_full, attn_panel, shares = gather_all(cell_rows, panels[0], panel_slot)
    normed = rms_scale(cell_full.astype(F32), attn_gain).astype(BF)
    projected = jnp.dot(
        normed, attn_panel[:, : 3 * HD], preferred_element_type=F32
    ).astype(BF)
    key_window = extended(projected[:, HD:], "wide", 2 * BLK)
    pair_blocks = key_window.reshape(block_count + 4, BLK, 2, HD)
    stacked = jnp.stack([pair_blocks[o : o + block_count] for o in range(5)], axis=1)
    query_index = (
        lax.axis_index("wide") * block_count
        + jnp.arange(block_count, dtype=jnp.int32)
        + block_count // 2
    ) % NET_BLOCKS
    allowed = block_mask(layout, query_index)
    queries = projected[:, :HD].reshape(block_count, BLK, HD)
    scores = jnp.einsum(
        "bqc,bokc->bqok", queries, stacked[:, :, :, 0, :], preferred_element_type=F32
    ) * HD ** (-0.5)
    lifted = jnp.where(allowed[:, None, :, None], jnp.exp(scores), F32(0.0))
    weights = (lifted / jnp.sum(lifted, axis=(2, 3), keepdims=True)).astype(BF)
    head_out = jnp.einsum(
        "bqok,bokc->bqc", weights, stacked[:, :, :, 1, :], preferred_element_type=F32
    ).astype(BF)
    partial_value = lax.dot_general(
        head_out.reshape(row_count, HD), attn_panel[:, 3 * HD :],
        (((1,), (1,)), ((), ())), preferred_element_type=F32,
    ).astype(BF)
    stream, stream_full, up_panel, down_panel = call_reduce_and_gather(
        partial_value, cell_rows, shares
    )
    normed_ffn = rms_scale(stream_full.astype(F32), ffn_gain).astype(BF)
    hidden = jax.nn.gelu(
        jnp.dot(normed_ffn, up_panel, preferred_element_type=F32), approximate=False
    ).astype(BF)
    ffn_part = lax.dot_general(
        hidden, down_panel, (((1,), (1,)), ((), ())), preferred_element_type=F32
    ).astype(BF)
    return call_reduce_only(ffn_part, stream)


def solution(mesh):
    return jax.shard_map(
        on_device,
        mesh=mesh,
        in_specs=(P("wide", "narrow"), P(), P(), P("wide", None, "narrow"), P(), P("wide", None)),
        out_specs=P("wide", "narrow"),
        check_vma=False,
    )
```
